512 devices in a mesh: seq: 64 (over x, z), head: 8 (over y, core).
Axes of the slice: x: 4, y: 4, z: 16, core: 2. Of those that a mesh axis runs over, the one named last changes fastest.
Arguments:
- queries: bfloat16 [16384, 8192], P('seq', 'head'), may hold values from -5 to 5
- key_rows: bfloat16 [16384, 8192], P('seq', 'head'), may hold values from -5 to 5
- values: bfloat16 [16384, 8192], P('seq', 'head'), may hold values from -6 to 6
- grad_out: bfloat16 [16384, 8192], P('seq', 'head'), may hold values from -6 to 6
- routes: int32 [64, 16384, 1], P('head', 'seq'), may hold values from 0 to 63; in each aligned block of 256 rows (0 to 255, 256 to 511, ..., all dimensions but the last counted through in order) at most 6 rows name the same one
Outputs:
- attended: bfloat16 [16384, 8192], P('seq', 'head')
- grad_query: bfloat16 [16384, 8192], P('seq', 'head')
- grad_key: bfloat16 [16384, 8192], P('seq', 'head')
- grad_value: bfloat16 [16384, 8192], P('seq', 'head')
The draws below stay inside these ranges and needn't reach their ends.
Inputs may be any that keep to these rules, and one draw needn't show every extreme that they name: `routes`: for each head, no cluster is named by more than 6 of the 256 tokens of one index of seq, a bound that some block reaches of them.
All inputs are finite; a program needn't handle non-finite values.
Results may differ from the reference program's by a relative error of at most 0.0029.
The reference program's roundings to bfloat16 on the way count: a program that leaves them out, or rounds other values in their place, can miss the bound.
Values may be sent and summed in bfloat16 or wider, within the bound.
No kernel may reach another device: no remote copies, remote signals or barrier semaphores. Data moves between devices by JAX's collectives and lax.ppermute only.
A program may use at most 64 MiB of HBM per device.

```python
import math
import jax
import jax.numpy as jnp
import numpy as np
from jax import lax

HEADS = 64
HD = 128
TOK_DEV = 256
TOKENS = 16384
CLUSTERS = 64
CAP = 6
N_SEQ = 64


def drawn_pair(key):
    base = jax.random.fold_in(key, 7)
    first, second = jax.random.split(base, 2)
    shape = (TOKENS, HEADS * HD)
    query_part = jnp.clip(jax.random.normal(first, shape, jnp.float32), -4.5, 4.5)
    key_part = jnp.clip(jax.random.normal(second, shape, jnp.float32), -4.5, 4.5)
    return (query_part, key_part)


def draw_queries(key, part):
    return drawn_pair(key)[0].astype(jnp.bfloat16)


def draw_key_rows(key, part):
    return drawn_pair(key)[1].astype(jnp.bfloat16)


def block_levels(key, shape, pieces, least, top_value):
    def one(axis_at, blocks):
        steps = jax.random.uniform(jax.random.fold_in(jax.random.fold_in(key, 6), axis_at), (blocks,), jnp.float32, least / len(pieces), top_value / len(pieces))
        return jnp.repeat(jnp.exp(steps), shape[axis_at] // blocks).reshape((-1,) + (1,) * (len(shape) - axis_at - 1))

    level = one(*pieces[0])
    for cut in pieces[1:]:
        level = level * one(*cut)
    return level


def deal_out(rng, own, number, rows, amount, top, bound, lean):
    order = jax.random.permutation(rng, amount)
    crowded, usual = portions_of(amount, rows * top, bound, lean, True), portions_of(amount, rows * top, bound, lean, False)
    places = jnp.arange(amount)

    def named(sizes, offset_by):
        used = int((sizes > 0).sum())
        fixed = max(1, used // 4)
        moved = fixed + (places - fixed + offset_by * (used - fixed)) % max(1, amount - fixed)
        return jnp.zeros((amount,), jnp.int32).at[order[jnp.where(places < fixed, places, moved)]].set(jnp.asarray(sizes, jnp.int32))

    sizes = jnp.where(number % 4 == 0, named(crowded, number // 4), named(usual, number - number // 4 - 1))
    mixed = jax.random.permutation(jax.random.fold_in(own, 3), amount)
    donor, sink = mixed[0:amount // 2 * 2:2], mixed[1:amount // 2 * 2:2]
    margin = jnp.minimum(sizes[donor] - 1, bound - sizes[sink]) // 2
    margin = jnp.where((donor == order[0]) | (sink == order[0]) | (sizes[sink] == 0), 0, jnp.maximum(margin, 0))
    moved = jax.random.randint(jax.random.fold_in(own, 4), (amount // 2,), 0, 1 << 20) % (margin + 1)
    sizes = sizes.at[donor].add(-moved).at[sink].add(moved)
    labels = jnp.searchsorted(jnp.cumsum(sizes), jnp.arange(rows * top), side="right").astype(jnp.int32)
    table = labels.reshape(top, rows).T
    table = table[jax.random.permutation(jax.random.fold_in(own, 1), rows)]
    offset_by = jax.random.randint(jax.random.fold_in(own, 2), (rows, 1), 0, top)
    return jnp.take_along_axis(table, (jnp.arange(top)[None, :] + offset_by) % top, axis=1)


def portions_of(number_of, total, reach, lean, full):
    loads = [(1 << 20) // math.isqrt(grade ** lean) + 1 for grade in range(1, number_of + 1)]
    largest = reach if full else min(reach, max(-(-total // number_of), total * loads[0] // sum(loads)))
    least = 1 if total - largest >= number_of - 1 else 0
    given, surplus = [largest] + [least] * (number_of - 1), total - largest - least * (number_of - 1)
    while surplus > 0:
        movable = [i for i in range(1, number_of) if given[i] < largest] or [i for i in range(1, number_of) if given[i] < reach]
        pool, remaining = sum([loads[i] for i in movable]), surplus
        for i in movable:
            extra = min(reach - given[i], max(1, remaining * loads[i] // pool), surplus)
            given[i] = given[i] + extra
            surplus = surplus - extra
    return np.array(given)


def centred(own_key, extent, scale, reach, shards=(), held_as=jnp.bfloat16):
    values = scale * jax.random.normal(own_key, extent, jnp.float32)
    if shards:
        values = values * block_levels(own_key, extent, shards, -0.22, 0.18)
    return jnp.clip(values, -reach, reach).astype(held_as)


def setup_inputs(seed: int = 0) -> dict:
    splits = jax.random.split(jax.random.key(seed), 6)
    queries = draw_queries(jax.random.fold_in(splits[5], 71), 0)
    key_rows = draw_key_rows(jax.random.fold_in(splits[5], 71), 0)
    values = centred(splits[2], (TOKENS, HEADS * HD), 1.0, 6.0, ((0, 64), (1, 8)))
    grad_out = centred(splits[3], (TOKENS, HEADS * HD), 1.0, 6.0, ((0, 64), (1, 8)))
    routes_keys = jax.random.split(jax.random.fold_in(splits[4], 1), HEADS * TOKENS // TOK_DEV)
    routes_turns = jax.random.permutation(jax.random.fold_in(splits[4], 3), HEADS * TOKENS // TOK_DEV)
    routes = jax.vmap(lambda own, number: deal_out(jax.random.fold_in(splits[4], 2), own, number, TOK_DEV, CLUSTERS, 1, CAP, 2))(routes_keys, routes_turns).reshape((HEADS, TOKENS, 1))
    return {"queries": queries, "key_rows": key_rows, "values": values, "grad_out": grad_out, "routes": routes}


def cluster_block(members):
    query_block, key_block, value_block, grad_block, live_keys = members
    scaling = 1.0 / math.sqrt(query_block.shape[1])
    scores = jnp.dot(query_block, key_block.T, preferred_element_type=jnp.float32) * scaling
    masked = jnp.where(live_keys[None, :], scores, -1e+30)
    row_peak = lax.optimization_barrier(jnp.max(masked, axis=1, keepdims=True))
    weights = jnp.exp(masked - row_peak)
    probability = weights / lax.optimization_barrier(jnp.sum(weights, axis=1, keepdims=True))
    probability_low = probability.astype(jnp.bfloat16)
    output = jnp.dot(probability_low, value_block, preferred_element_type=jnp.float32).astype(jnp.bfloat16)
    grad_probability = jnp.dot(grad_block, value_block.T, preferred_element_type=jnp.float32)
    delta_rows = lax.optimization_barrier(jnp.sum(grad_block.astype(jnp.float32) * output.astype(jnp.float32), axis=1, keepdims=True))
    grad_scores = (probability * (grad_probability - delta_rows)).astype(jnp.bfloat16)
    grad_query = (jnp.dot(grad_scores, key_block, preferred_element_type=jnp.float32) * scaling).astype(jnp.bfloat16)
    grad_key = (jnp.dot(grad_scores.T, query_block, preferred_element_type=jnp.float32) * scaling).astype(jnp.bfloat16)
    grad_value = jnp.dot(probability_low.T, grad_block, preferred_element_type=jnp.float32).astype(jnp.bfloat16)
    return (output, grad_query, grad_key, grad_value)

def reference(queries, key_rows, values, grad_out, routes):
    row_count = N_SEQ * CAP

    def split_heads(tensor):
        return tensor.reshape(TOKENS, HEADS, HD).transpose(1, 0, 2)

    def one_head(members):
        query_head, key_head, value_head, grad_head, cluster = members
        onehot = (cluster[:, None] == jnp.arange(N_SEQ, dtype=jnp.int32)[None, :]).astype(jnp.int32)
        blocks = onehot.reshape(N_SEQ, TOK_DEV, N_SEQ)
        before = (jnp.cumsum(blocks, axis=1) - blocks).reshape(TOKENS, N_SEQ)
        ranking = lax.optimization_barrier(jnp.sum(before * onehot, axis=1)).astype(jnp.int32)
        source = (jnp.arange(TOKENS, dtype=jnp.int32) // TOK_DEV).astype(jnp.int32)
        placing = (cluster * row_count + source * CAP + ranking).astype(jnp.int32)

        def spread(tensor):
            empty = jnp.zeros((N_SEQ * row_count, HD), tensor.dtype)
            return empty.at[placing].set(tensor).reshape(N_SEQ, row_count, HD)
        live = jnp.zeros((N_SEQ * row_count,), jnp.bool_).at[placing].set(True).reshape(N_SEQ, row_count)
        results = lax.map(cluster_block, (spread(query_head), spread(key_head), spread(value_head), spread(grad_head), live))
        return tuple((result.reshape(N_SEQ * row_count, HD)[placing] for result in results))
    outputs = lax.map(one_head, (split_heads(queries), split_heads(key_rows), split_heads(values), split_heads(grad_out), routes[:, :, 0]))
    return tuple((result.transpose(1, 0, 2).reshape(TOKENS, HEADS * HD) for result in outputs))
```

```python
import math

import jax
import jax.numpy as jnp
from jax import lax
from jax.experimental import pallas as pl
from jax.experimental.pallas import tpu as pltpu
from jax.sharding import PartitionSpec as P

DEAD_KEY = 256.0
DEAD_TEST = 100.0


def dot_nn(left, right):
    return jnp.dot(left, right, preferred_element_type=jnp.float32)


def dot_nt(left, right):
    return lax.dot_general(left, right, (((1,), (1,)), ((), ())), preferred_element_type=jnp.float32)


def dot_tn(left, right):
    return lax.dot_general(left, right, (((0,), (0,)), ((), ())), preferred_element_type=jnp.float32)


def pack_kernel(routes_ref, q_ref, k_ref, v_ref, g_ref, out_ref, place_ref, scratch, *, owners, slots):
    tokens = routes_ref.shape[2]
    rows = owners * slots
    clusters = routes_ref[0]
    onehot = lax.broadcasted_iota(jnp.int32, (owners, tokens), 0) == clusters
    onehot_low = jnp.where(onehot, 1.0, 0.0).astype(jnp.bfloat16)
    earlier = lax.broadcasted_iota(jnp.int32, (tokens, tokens), 0) < lax.broadcasted_iota(
        jnp.int32, (tokens, tokens), 1
    )
    before = dot_nn(onehot_low, jnp.where(earlier, 1.0, 0.0).astype(jnp.bfloat16))
    ranking = jnp.sum(jnp.where(onehot, before, 0.0), axis=0, keepdims=True)
    place = clusters * slots + ranking.astype(jnp.int32)
    place_ref[0] = place
    select = jnp.where(
        lax.broadcasted_iota(jnp.int32, (rows, tokens), 0) == place, 1.0, 0.0
    ).astype(jnp.bfloat16)
    size = q_ref.shape[1]
    query_key = dot_nn(select, jnp.concatenate([q_ref[...], k_ref[...]], axis=1))
    value_grad = dot_nn(select, jnp.concatenate([v_ref[...], g_ref[...]], axis=1))
    live = dot_nn(select, jnp.ones((tokens, size), jnp.bfloat16))
    scratch[pl.ds(0, rows, stride=4), :] = query_key[:, :size]
    scratch[pl.ds(1, rows, stride=4), :] = query_key[:, size:] + (1.0 - live) * DEAD_KEY
    scratch[pl.ds(2, rows, stride=4), :] = value_grad[:, :size]
    scratch[pl.ds(3, rows, stride=4), :] = value_grad[:, size:]
    out_ref[...] = scratch[...].astype(jnp.bfloat16)


def attention_kernel(in_ref, out_ref, scratch):
    rows = in_ref.shape[0] // 4
    size = in_ref.shape[1]
    scaling = 1.0 / math.sqrt(size)
    scratch[...] = in_ref[...].astype(jnp.float32)
    query, key, value, grad = [
        scratch[pl.ds(i, rows, stride=4), :].astype(jnp.bfloat16) for i in range(4)
    ]
    first_lane = jnp.where(lax.broadcasted_iota(jnp.int32, (8, size), 1) == 0, 1.0, 0.0)
    marks = dot_nt(first_lane.astype(jnp.bfloat16), key)[0:1]
    scores = dot_nt(query, key) * scaling
    masked = jnp.where(marks < DEAD_TEST, scores, -1e30)
    weights = jnp.exp(masked - jnp.max(masked, axis=1, keepdims=True))
    probability = weights * (1.0 / jnp.sum(weights, axis=1, keepdims=True))
    probability_low = probability.astype(jnp.bfloat16)
    output = dot_nn(probability_low, value).astype(jnp.bfloat16)
    grad_probability = dot_nt(grad, value)
    delta = jnp.sum(
        grad.astype(jnp.float32) * output.astype(jnp.float32), axis=1, keepdims=True
    )
    grad_scores = (probability * (grad_probability - delta)).astype(jnp.bfloat16)
    scratch[pl.ds(0, rows, stride=4), :] = output.astype(jnp.float32)
    scratch[pl.ds(1, rows, stride=4), :] = dot_nn(grad_scores, key) * scaling
    scratch[pl.ds(2, rows, stride=4), :] = dot_tn(grad_scores, query) * scaling
    scratch[pl.ds(3, rows, stride=4), :] = dot_tn(probability_low, grad)
    out_ref[...] = scratch[...].astype(jnp.bfloat16)


def unpack_kernel(place_ref, in_ref, o_ref, dq_ref, dk_ref, dv_ref, scratch):
    rows = in_ref.shape[0] // 4
    tokens, size = o_ref.shape
    scratch[...] = in_ref[...].astype(jnp.float32)
    select = jnp.where(
        lax.broadcasted_iota(jnp.int32, (rows, tokens), 0) == place_ref[0], 1.0, 0.0
    ).astype(jnp.bfloat16)
    parts = [scratch[pl.ds(i, rows, stride=4), :].astype(jnp.bfloat16) for i in range(4)]
    first = dot_tn(select, jnp.concatenate(parts[:2], axis=1)).astype(jnp.bfloat16)
    second = dot_tn(select, jnp.concatenate(parts[2:], axis=1)).astype(jnp.bfloat16)
    o_ref[...] = first[:, :size]
    dq_ref[...] = first[:, size:]
    dk_ref[...] = second[:, :size]
    dv_ref[...] = second[:, size:]


def body(queries, key_rows, values, grad_out, routes):
    tokens, features = queries.shape
    heads = routes.shape[0]
    size = features // heads
    owners = lax.axis_size("seq")
    slots = 3 * tokens // (2 * owners)
    rows = owners * slots
    params = pltpu.CompilerParams(
        dimension_semantics=("arbitrary",), vmem_limit_bytes=48 * 1024 * 1024
    )
    head_rows = pl.BlockSpec((tokens, size), lambda h: (0, h))
    head_row = pl.BlockSpec((1, 1, tokens), lambda h: (h, 0, 0))
    packed_block = pl.BlockSpec((4 * rows, size), lambda h: (0, h))
    packed_shape = jax.ShapeDtypeStruct((4 * rows, features), jnp.bfloat16)
    scratch = [pltpu.VMEM((4 * rows, size), jnp.float32)]

    def exchange(packed):
        moved = lax.all_to_all(
            packed.reshape(owners, 4 * slots, features), "seq", split_axis=0, concat_axis=0, tiled=True
        )
        return moved.reshape(4 * rows, features)

    packed, place = pl.pallas_call(
        lambda *refs: pack_kernel(*refs, owners=owners, slots=slots),
        grid=(heads,),
        in_specs=[head_row, head_rows, head_rows, head_rows, head_rows],
        out_specs=[packed_block, head_row],
        out_shape=[packed_shape, jax.ShapeDtypeStruct((heads, 1, tokens), jnp.int32)],
        scratch_shapes=scratch,
        compiler_params=params,
        name="pack_rows",
    )(routes.reshape(heads, 1, tokens), queries, key_rows, values, grad_out)
    results = pl.pallas_call(
        attention_kernel,
        grid=(heads,),
        in_specs=[packed_block],
        out_specs=packed_block,
        out_shape=packed_shape,
        scratch_shapes=scratch,
        compiler_params=params,
        name="cluster_attention",
    )(exchange(packed))
    return tuple(
        pl.pallas_call(
            unpack_kernel,
            grid=(heads,),
            in_specs=[head_row, packed_block],
            out_specs=[head_rows] * 4,
            out_shape=[jax.ShapeDtypeStruct((tokens, features), jnp.bfloat16)] * 4,
            scratch_shapes=scratch,
            compiler_params=params,
            name="unpack_rows",
        )(place, exchange(results))
    )


def solution(mesh):
    in_specs = (
        P("seq", "head"),
        P("seq", "head"),
        P("seq", "head"),
        P("seq", "head"),
        P("head", "seq", None),
    )
    out_specs = (P("seq", "head"), P("seq", "head"), P("seq", "head"), P("seq", "head"))
    return jax.shard_map(body, mesh=mesh, in_specs=in_specs, out_specs=out_specs, check_vma=False)
```

```python
import math

import jax
import jax.numpy as jnp
from jax import lax
from jax.experimental import pallas as pl
from jax.experimental.pallas import tpu as pltpu
from jax.sharding import PartitionSpec as P

DEAD_KEY = 256.0
DEAD_TEST = 100.0
PACK_HEADS = 4
ATTEND_HEADS = 2
UNPACK_HEADS = 4


def dot_nn(left, right):
    return jnp.dot(left, right, preferred_element_type=jnp.float32)


def dot_nt(left, right):
    return lax.dot_general(left, right, (((1,), (1,)), ((), ())), preferred_element_type=jnp.float32)


def dot_tn(left, right):
    return lax.dot_general(left, right, (((0,), (0,)), ((), ())), preferred_element_type=jnp.float32)


def pack_kernel(routes_ref, q_ref, k_ref, v_ref, g_ref, out_ref, place_ref, scratch, *, owners, slots):
    group, _, tokens = routes_ref.shape
    rows = owners * slots
    size = q_ref.shape[1] // group
    earlier = lax.broadcasted_iota(jnp.int32, (tokens, tokens), 0) < lax.broadcasted_iota(
        jnp.int32, (tokens, tokens), 1
    )
    earlier_low = jnp.where(earlier, 1.0, 0.0).astype(jnp.bfloat16)
    owner_ids = lax.broadcasted_iota(jnp.int32, (owners, tokens), 0)
    row_ids = lax.broadcasted_iota(jnp.int32, (rows, tokens), 0)
    for j in range(group):
        lanes = slice(j * size, (j + 1) * size)
        clusters = routes_ref[j]
        onehot = owner_ids == clusters
        before = dot_nn(jnp.where(onehot, 1.0, 0.0).astype(jnp.bfloat16), earlier_low)
        ranking = jnp.sum(jnp.where(onehot, before, 0.0), axis=0, keepdims=True)
        place = clusters * slots + ranking.astype(jnp.int32)
        place_ref[j] = place
        select = jnp.where(row_ids == place, 1.0, 0.0).astype(jnp.bfloat16)
        query_key = dot_nn(select, jnp.concatenate([q_ref[:, lanes], k_ref[:, lanes]], axis=1))
        value_grad = dot_nn(select, jnp.concatenate([v_ref[:, lanes], g_ref[:, lanes]], axis=1))
        live = dot_nn(select, jnp.ones((tokens, size), jnp.bfloat16))
        scratch[j, pl.ds(0, rows, stride=4), :] = query_key[:, :size]
        scratch[j, pl.ds(1, rows, stride=4), :] = query_key[:, size:] + (1.0 - live) * DEAD_KEY
        scratch[j, pl.ds(2, rows, stride=4), :] = value_grad[:, :size]
        scratch[j, pl.ds(3, rows, stride=4), :] = value_grad[:, size:]
        out_ref[:, lanes] = scratch[j].astype(jnp.bfloat16)


def attention_kernel(in_ref, out_ref, scratch, scratch_out):
    rows = in_ref.shape[0] // 4
    group = scratch.shape[0]
    size = in_ref.shape[1] // group
    scaling = 1.0 / math.sqrt(size)
    first_lane = jnp.where(lax.broadcasted_iota(jnp.int32, (8, size), 1) == 0, 1.0, 0.0)
    first_lane = first_lane.astype(jnp.bfloat16)
    for j in range(group):
        lanes = slice(j * size, (j + 1) * size)
        scratch[j] = in_ref[:, lanes].astype(jnp.float32)
        query, key, value, grad = [
            scratch[j, pl.ds(i, rows, stride=4), :].astype(jnp.bfloat16) for i in range(4)
        ]
        marks = dot_nt(first_lane, key)[0:1]
        scores = dot_nt(query, key) * scaling
        masked = jnp.where(marks < DEAD_TEST, scores, -1e30)
        weights = jnp.exp(masked - jnp.max(masked, axis=1, keepdims=True))
        probability = weights * (1.0 / jnp.sum(weights, axis=1, keepdims=True))
        probability_low = probability.astype(jnp.bfloat16)
        output = dot_nn(probability_low, value).astype(jnp.bfloat16)
        grad_probability = dot_nt(grad, value)
        delta = jnp.sum(
            grad.astype(jnp.float32) * output.astype(jnp.float32), axis=1, keepdims=True
        )
        grad_scores = (probability * (grad_probability - delta)).astype(jnp.bfloat16)
        scratch_out[j, pl.ds(0, rows, stride=4), :] = output.astype(jnp.float32)
        scratch_out[j, pl.ds(1, rows, stride=4), :] = dot_nn(grad_scores, key) * scaling
        scratch_out[j, pl.ds(2, rows, stride=4), :] = dot_tn(grad_scores, query) * scaling
        scratch_out[j, pl.ds(3, rows, stride=4), :] = dot_tn(probability_low, grad)
        out_ref[:, lanes] = scratch_out[j].astype(jnp.bfloat16)


def unpack_kernel(place_ref, in_ref, o_ref, dq_ref, dk_ref, dv_ref, scratch):
    rows = in_ref.shape[0] // 4
    group, _, tokens = place_ref.shape
    size = o_ref.shape[1] // group
    row_ids = lax.broadcasted_iota(jnp.int32, (rows, tokens), 0)
    for j in range(group):
        lanes = slice(j * size, (j + 1) * size)
        scratch[j] = in_ref[:, lanes].astype(jnp.float32)
        select = jnp.where(row_ids == place_ref[j], 1.0, 0.0).astype(jnp.bfloat16)
        parts = [scratch[j, pl.ds(i, rows, stride=4), :].astype(jnp.bfloat16) for i in range(4)]
        first = dot_tn(select, jnp.concatenate(parts[:2], axis=1)).astype(jnp.bfloat16)
        second = dot_tn(select, jnp.concatenate(parts[2:], axis=1)).astype(jnp.bfloat16)
        o_ref[:, lanes] = first[:, :size]
        dq_ref[:, lanes] = first[:, size:]
        dk_ref[:, lanes] = second[:, :size]
        dv_ref[:, lanes] = second[:, size:]


def build(tokens, features, heads, owners):
    size = features // heads
    slots = 3 * tokens // (2 * owners)
    rows = owners * slots
    params = pltpu.CompilerParams(
        dimension_semantics=("arbitrary",), vmem_limit_bytes=56 * 1024 * 1024
    )
    packed_shape = jax.ShapeDtypeStruct((4 * rows, features), jnp.bfloat16)

    def head_rows(group):
        return pl.BlockSpec((tokens, group * size), lambda h: (0, h))

    def head_row(group):
        return pl.BlockSpec((group, 1, tokens), lambda h: (h, 0, 0))

    def packed_block(group):
        return pl.BlockSpec((4 * rows, group * size), lambda h: (0, h))

    def scratch(group):
        return pltpu.VMEM((group, 4 * rows, size), jnp.float32)

    pack = pl.pallas_call(
        lambda *refs: pack_kernel(*refs, owners=owners, slots=slots),
        grid=(heads // PACK_HEADS,),
        in_specs=[head_row(PACK_HEADS)] + [head_rows(PACK_HEADS)] * 4,
        out_specs=[packed_block(PACK_HEADS), head_row(PACK_HEADS)],
        out_shape=[packed_shape, jax.ShapeDtypeStruct((heads, 1, tokens), jnp.int32)],
        scratch_shapes=[scratch(PACK_HEADS)],
        compiler_params=params,
        name="pack_rows",
    )
    attend = pl.pallas_call(
        attention_kernel,
        grid=(heads // ATTEND_HEADS,),
        in_specs=[packed_block(ATTEND_HEADS)],
        out_specs=packed_block(ATTEND_HEADS),
        out_shape=packed_shape,
        scratch_shapes=[scratch(ATTEND_HEADS)] * 2,
        compiler_params=params,
        name="cluster_attention",
    )
    unpack = pl.pallas_call(
        unpack_kernel,
        grid=(heads // UNPACK_HEADS,),
        in_specs=[head_row(UNPACK_HEADS), packed_block(UNPACK_HEADS)],
        out_specs=[head_rows(UNPACK_HEADS)] * 4,
        out_shape=[jax.ShapeDtypeStruct((tokens, features), jnp.bfloat16)] * 4,
        scratch_shapes=[scratch(UNPACK_HEADS)],
        compiler_params=params,
        name="unpack_rows",
    )
    return pack, attend, unpack


def body(queries, key_rows, values, grad_out, routes):
    tokens, features = queries.shape
    heads = routes.shape[0]
    owners = lax.axis_size("seq")
    pack, attend, unpack = build(tokens, features, heads, owners)

    def exchange(packed):
        moved = lax.all_to_all(
            packed.reshape(owners, -1, features), "seq", split_axis=0, concat_axis=0, tiled=True
        )
        return moved.reshape(packed.shape)

    def in_hbm(array):
        return pltpu.with_memory_space_constraint(array, pltpu.HBM)

    packed, place = pack(
        routes.reshape(heads, 1, tokens),
        in_hbm(queries),
        in_hbm(key_rows),
        in_hbm(values),
        in_hbm(grad_out),
    )
    results = attend(exchange(packed))
    return tuple(unpack(place, exchange(results)))


def solution(mesh):
    in_specs = (
        P("seq", "head"),
        P("seq", "head"),
        P("seq", "head"),
        P("seq", "head"),
        P("head", "seq", None),
    )
    out_specs = (P("seq", "head"), P("seq", "head"), P("seq", "head"), P("seq", "head"))
    return jax.shard_map(body, mesh=mesh, in_specs=in_specs, out_specs=out_specs, check_vma=False)
```

```python
import math

import jax
import jax.numpy as jnp
from jax import lax
from jax.experimental import pallas as pl
from jax.experimental.pallas import tpu as pltpu
from jax.sharding import PartitionSpec as P

DEAD_KEY = 256.0
DEAD_TEST = 100.0
MESSAGE_ROWS = 44
OWNED = 8
WIDE = 8
SOURCES = 4
PACK_HEADS = 4
ATTEND_HEADS = 2
UNPACK_HEADS = 4


def dot_nn(left, right):
    return jnp.dot(left, right, preferred_element_type=jnp.float32)


def dot_nt(left, right):
    return lax.dot_general(left, right, (((1,), (1,)), ((), ())), preferred_element_type=jnp.float32)


def dot_tn(left, right):
    return lax.dot_general(left, right, (((0,), (0,)), ((), ())), preferred_element_type=jnp.float32)


def pack_kernel(routes_ref, q_ref, k_ref, v_ref, g_ref, out_ref, place_ref, scratch, *, owners, slots):
    group, _, tokens = routes_ref.shape
    rows = owners * slots
    size = q_ref.shape[1] // group
    earlier = lax.broadcasted_iota(jnp.int32, (tokens, tokens), 0) < lax.broadcasted_iota(
        jnp.int32, (tokens, tokens), 1
    )
    earlier_low = jnp.where(earlier, 1.0, 0.0).astype(jnp.bfloat16)
    owner_ids = lax.broadcasted_iota(jnp.int32, (owners, tokens), 0)
    row_ids = lax.broadcasted_iota(jnp.int32, (rows, tokens), 0)
    for j in range(group):
        lanes = slice(j * size, (j + 1) * size)
        clusters = routes_ref[j]
        onehot = owner_ids == clusters
        before = dot_nn(jnp.where(onehot, 1.0, 0.0).astype(jnp.bfloat16), earlier_low)
        ranking = jnp.sum(jnp.where(onehot, before, 0.0), axis=0, keepdims=True)
        place = clusters * slots + ranking.astype(jnp.int32)
        place_ref[j] = place
        select = jnp.where(row_ids == place, 1.0, 0.0).astype(jnp.bfloat16)
        query_key = dot_nn(select, jnp.concatenate([q_ref[:, lanes], k_ref[:, lanes]], axis=1))
        value_grad = dot_nn(select, jnp.concatenate([v_ref[:, lanes], g_ref[:, lanes]], axis=1))
        live = dot_nn(select, jnp.ones((tokens, size), jnp.bfloat16))
        scratch[j, pl.ds(0, rows, stride=4), :] = query_key[:, :size]
        scratch[j, pl.ds(1, rows, stride=4), :] = query_key[:, size:] + (1.0 - live) * DEAD_KEY
        scratch[j, pl.ds(2, rows, stride=4), :] = value_grad[:, :size]
        scratch[j, pl.ds(3, rows, stride=4), :] = value_grad[:, size:]
        out_ref[:, lanes] = scratch[j].astype(jnp.bfloat16)


def attend_cluster(query, key, value, grad):
    size = query.shape[1]
    scaling = 1.0 / math.sqrt(size)
    first_lane = jnp.where(lax.broadcasted_iota(jnp.int32, (8, size), 1) == 0, 1.0, 0.0)
    marks = dot_nt(first_lane.astype(jnp.bfloat16), key)[0:1]
    scores = dot_nt(query, key) * scaling
    masked = jnp.where(marks < DEAD_TEST, scores, -1e30)
    weights = jnp.exp(masked - jnp.max(masked, axis=1, keepdims=True))
    probability = weights * (1.0 / jnp.sum(weights, axis=1, keepdims=True))
    probability_low = probability.astype(jnp.bfloat16)
    output = dot_nn(probability_low, value).astype(jnp.bfloat16).astype(jnp.float32)
    grad_probability = dot_nt(grad, value)
    delta = jnp.sum(grad.astype(jnp.float32) * output, axis=1, keepdims=True)
    grad_scores = (probability * (grad_probability - delta)).astype(jnp.bfloat16)
    return (
        output,
        dot_nn(grad_scores, key) * scaling,
        dot_tn(grad_scores, query) * scaling,
        dot_tn(probability_low, grad),
    )


def attention_kernel(in_ref, out_ref, scratch, scratch_out):
    rows = in_ref.shape[0] // 4
    group = scratch.shape[0]
    size = in_ref.shape[1] // group
    for j in range(group):
        lanes = slice(j * size, (j + 1) * size)
        scratch[j] = in_ref[:, lanes].astype(jnp.float32)
        tensors = [scratch[j, pl.ds(i, rows, stride=4), :].astype(jnp.bfloat16) for i in range(4)]
        for i, result in enumerate(attend_cluster(*tensors)):
            scratch_out[j, pl.ds(i, rows, stride=4), :] = result
        out_ref[:, lanes] = scratch_out[j].astype(jnp.bfloat16)


def unpack_kernel(place_ref, in_ref, o_ref, dq_ref, dk_ref, dv_ref, scratch):
    rows = in_ref.shape[0] // 4
    group, _, tokens = place_ref.shape
    size = o_ref.shape[1] // group
    row_ids = lax.broadcasted_iota(jnp.int32, (rows, tokens), 0)
    for j in range(group):
        lanes = slice(j * size, (j + 1) * size)
        scratch[j] = in_ref[:, lanes].astype(jnp.float32)
        select = jnp.where(row_ids == place_ref[j], 1.0, 0.0).astype(jnp.bfloat16)
        parts = [scratch[j, pl.ds(i, rows, stride=4), :].astype(jnp.bfloat16) for i in range(4)]
        first = dot_tn(select, jnp.concatenate(parts[:2], axis=1)).astype(jnp.bfloat16)
        second = dot_tn(select, jnp.concatenate(parts[2:], axis=1)).astype(jnp.bfloat16)
        o_ref[:, lanes] = first[:, :size]
        dq_ref[:, lanes] = first[:, size:]
        dk_ref[:, lanes] = second[:, :size]
        dv_ref[:, lanes] = second[:, size:]


def dense_pack_kernel(
    routes_ref, q_ref, k_ref, v_ref, g_ref, out_ref, place_ref, counts_ref, scratch, *, clusters
):
    group, _, tokens = routes_ref.shape
    rows = scratch.shape[1] // 4
    size = q_ref.shape[1] // group
    earlier = lax.broadcasted_iota(jnp.int32, (tokens, tokens), 0) < lax.broadcasted_iota(
        jnp.int32, (tokens, tokens), 1
    )
    earlier_low = jnp.where(earlier, 1.0, 0.0).astype(jnp.bfloat16)
    this = lax.broadcasted_iota(jnp.int32, (clusters, clusters), 0)
    other = lax.broadcasted_iota(jnp.int32, (clusters, clusters), 1)
    lower = jnp.logical_and(other < this, other // OWNED == this // OWNED)
    lower_low = jnp.where(lower, 1.0, 0.0).astype(jnp.bfloat16)
    all_tokens = jnp.ones((tokens, tokens), jnp.bfloat16)
    cluster_ids = lax.broadcasted_iota(jnp.int32, (clusters, tokens), 0)
    row_ids = lax.broadcasted_iota(jnp.int32, (rows, tokens), 0)
    for j in range(group):
        lanes = slice(j * size, (j + 1) * size)
        route = routes_ref[j]
        onehot = cluster_ids == route
        onehot_low = jnp.where(onehot, 1.0, 0.0).astype(jnp.bfloat16)
        counts_ref[j] = dot_nt(all_tokens[:8], onehot_low)[0:1].astype(jnp.int32)
        in_lower = dot_nn(lower_low, onehot_low).astype(jnp.bfloat16)
        before = dot_nn(onehot_low, earlier_low) + dot_nn(in_lower, all_tokens)
        ranking = jnp.sum(jnp.where(onehot, before, 0.0), axis=0, keepdims=True)
        place = route // OWNED * MESSAGE_ROWS + ranking.astype(jnp.int32)
        place_ref[j] = place
        select = jnp.where(row_ids == place, 1.0, 0.0).astype(jnp.bfloat16)
        query_key = dot_nn(select, jnp.concatenate([q_ref[:, lanes], k_ref[:, lanes]], axis=1))
        value_grad = dot_nn(select, jnp.concatenate([v_ref[:, lanes], g_ref[:, lanes]], axis=1))
        scratch[j, pl.ds(0, rows, stride=4), :] = query_key[:, :size]
        scratch[j, pl.ds(1, rows, stride=4), :] = query_key[:, size:]
        scratch[j, pl.ds(2, rows, stride=4), :] = value_grad[:, :size]
        scratch[j, pl.ds(3, rows, stride=4), :] = value_grad[:, size:]
        out_ref[j * 4 * rows : (j + 1) * 4 * rows, :] = scratch[j].astype(jnp.bfloat16)


def dense_attention_kernel(counts_ref, in_ref, out_ref, target_ref, stage, wide_ref):
    size = in_ref.shape[1]
    steps, pairs = counts_ref.shape
    count = SOURCES * MESSAGE_ROWS
    wide = pairs * WIDE
    sources = steps * SOURCES
    slots = wide_ref.shape[1] // (sources * OWNED) - 2
    lanes = lax.broadcasted_iota(jnp.int32, (pairs, wide), 1) // WIDE
    pair = lax.broadcasted_iota(jnp.int32, (pairs, wide), 0)
    counts_low = counts_ref[...].astype(jnp.bfloat16)
    same = jnp.where(lanes == pair, 1.0, 0.0).astype(jnp.bfloat16)
    ahead = jnp.logical_and(pair < lanes, pair // OWNED == lanes // OWNED)
    ahead = jnp.where(ahead, 1.0, 0.0).astype(jnp.bfloat16)
    lane = lax.broadcasted_iota(jnp.int32, (steps, wide), 1)
    slot = lane % WIDE
    target = dot_nn(counts_low, ahead).astype(jnp.int32) + slot
    target = target + lane // (OWNED * WIDE) * MESSAGE_ROWS
    target_ref[...] = jnp.where(slot < dot_nn(counts_low, same).astype(jnp.int32), target, -1)
    row_ids = lax.broadcasted_iota(jnp.int32, (count, wide), 0)
    ones = jnp.ones((count, size), jnp.bfloat16)

    def selection(step):
        return jnp.where(row_ids == target_ref[pl.ds(step, 1), :], 1.0, 0.0).astype(jnp.bfloat16)

    def expand(pass_id, carry):
        for u in range(stage.shape[0]):
            step = pass_id * stage.shape[0] + u
            stage[u] = in_ref[pl.ds(step * 4 * count, 4 * count), :].astype(jnp.float32)
            parts = [stage[u, pl.ds(i, count, stride=4), :].astype(jnp.bfloat16) for i in range(4)]
            select = selection(step)
            into = pl.ds(step * wide, wide)
            query_key = dot_tn(select, jnp.concatenate(parts[:2], axis=1))
            value_grad = dot_tn(select, jnp.concatenate(parts[2:], axis=1))
            live = dot_tn(select, ones)
            wide_ref[0, into, :] = query_key[:, :size]
            wide_ref[1, into, :] = query_key[:, size:] + (1.0 - live) * DEAD_KEY
            wide_ref[2, into, :] = value_grad[:, :size]
            wide_ref[3, into, :] = value_grad[:, size:]
        return carry

    def compact(pass_id, carry):
        for u in range(stage.shape[0]):
            step = pass_id * stage.shape[0] + u
            select = selection(step)
            parts = [
                wide_ref[i, pl.ds(step * wide, wide), :].astype(jnp.bfloat16) for i in range(4)
            ]
            first = dot_nn(select, jnp.concatenate(parts[:2], axis=1))
            second = dot_nn(select, jnp.concatenate(parts[2:], axis=1))
            stage[u, pl.ds(0, count, stride=4), :] = first[:, :size]
            stage[u, pl.ds(1, count, stride=4), :] = first[:, size:]
            stage[u, pl.ds(2, count, stride=4), :] = second[:, :size]
            stage[u, pl.ds(3, count, stride=4), :] = second[:, size:]
            out_ref[pl.ds(step * 4 * count, 4 * count), :] = stage[u].astype(jnp.bfloat16)
        return carry

    lax.fori_loop(0, steps // stage.shape[0], expand, 0)
    for c in range(OWNED):
        spots = [pl.ds(c * WIDE + s, sources, stride=OWNED * WIDE) for s in range(slots)]
        tensors = [
            jnp.concatenate([wide_ref[i, spot, :] for spot in spots], axis=0).astype(jnp.bfloat16)
            for i in range(4)
        ]
        for i, result in enumerate(attend_cluster(*tensors)):
            for s, spot in enumerate(spots):
                wide_ref[i, spot, :] = result[s * sources : (s + 1) * sources]
    lax.fori_loop(0, steps // stage.shape[0], compact, 0)


def dense_unpack_kernel(place_ref, in_ref, o_ref, dq_ref, dk_ref, dv_ref, scratch):
    rows = scratch.shape[1] // 4
    group, _, tokens = place_ref.shape
    size = o_ref.shape[1] // group
    row_ids = lax.broadcasted_iota(jnp.int32, (rows, tokens), 0)
    for j in range(group):
        lanes = slice(j * size, (j + 1) * size)
        scratch[j] = in_ref[j * 4 * rows : (j + 1) * 4 * rows, :].astype(jnp.float32)
        select = jnp.where(row_ids == place_ref[j], 1.0, 0.0).astype(jnp.bfloat16)
        parts = [scratch[j, pl.ds(i, rows, stride=4), :].astype(jnp.bfloat16) for i in range(4)]
        first = dot_tn(select, jnp.concatenate(parts[:2], axis=1)).astype(jnp.bfloat16)
        second = dot_tn(select, jnp.concatenate(parts[2:], axis=1)).astype(jnp.bfloat16)
        o_ref[:, lanes] = first[:, :size]
        dq_ref[:, lanes] = first[:, size:]
        dk_ref[:, lanes] = second[:, :size]
        dv_ref[:, lanes] = second[:, size:]


def build(tokens, features, heads, owners):
    size = features // heads
    slots = 3 * tokens // (2 * owners)
    rows = owners * slots
    params = pltpu.CompilerParams(
        dimension_semantics=("arbitrary",), vmem_limit_bytes=40 * 1024 * 1024
    )
    packed_shape = jax.ShapeDtypeStruct((4 * rows, features), jnp.bfloat16)

    def head_rows(group):
        return pl.BlockSpec((tokens, group * size), lambda h: (0, h))

    def head_row(group):
        return pl.BlockSpec((group, 1, tokens), lambda h: (h, 0, 0))

    def packed_block(group):
        return pl.BlockSpec((4 * rows, group * size), lambda h: (0, h))

    def scratch(group):
        return pltpu.VMEM((group, 4 * rows, size), jnp.float32)

    pack = pl.pallas_call(
        lambda *refs: pack_kernel(*refs, owners=owners, slots=slots),
        grid=(heads // PACK_HEADS,),
        in_specs=[head_row(PACK_HEADS)] + [head_rows(PACK_HEADS)] * 4,
        out_specs=[packed_block(PACK_HEADS), head_row(PACK_HEADS)],
        out_shape=[packed_shape, jax.ShapeDtypeStruct((heads, 1, tokens), jnp.int32)],
        scratch_shapes=[scratch(PACK_HEADS)],
        compiler_params=params,
        name="pack_rows",
    )
    attend = pl.pallas_call(
        attention_kernel,
        grid=(heads // ATTEND_HEADS,),
        in_specs=[packed_block(ATTEND_HEADS)],
        out_specs=packed_block(ATTEND_HEADS),
        out_shape=packed_shape,
        scratch_shapes=[scratch(ATTEND_HEADS)] * 2,
        compiler_params=params,
        name="cluster_attention",
    )
    unpack = pl.pallas_call(
        unpack_kernel,
        grid=(heads // UNPACK_HEADS,),
        in_specs=[head_row(UNPACK_HEADS), packed_block(UNPACK_HEADS)],
        out_specs=[head_rows(UNPACK_HEADS)] * 4,
        out_shape=[jax.ShapeDtypeStruct((tokens, features), jnp.bfloat16)] * 4,
        scratch_shapes=[scratch(UNPACK_HEADS)],
        compiler_params=params,
        name="unpack_rows",
    )
    return pack, attend, unpack


def build_dense(tokens, features, heads, owners):
    size = features // heads
    clusters = heads * OWNED
    rows = OWNED * MESSAGE_ROWS
    slots = 3 * tokens // (2 * owners)
    steps = owners // SOURCES
    params = pltpu.CompilerParams(
        dimension_semantics=("arbitrary",), vmem_limit_bytes=40 * 1024 * 1024
    )
    packed_shape = jax.ShapeDtypeStruct((heads * 4 * rows, size), jnp.bfloat16)

    def head_rows(group):
        return pl.BlockSpec((tokens, group * size), lambda h: (0, h))

    def head_row(group, length):
        return pl.BlockSpec((group, 1, length), lambda h: (h, 0, 0))

    def packed_block(group):
        return pl.BlockSpec((group * 4 * rows, size), lambda h: (h, 0))

    def scratch(group):
        return pltpu.VMEM((group, 4 * rows, size), jnp.float32)

    pack = pl.pallas_call(
        lambda *refs: dense_pack_kernel(*refs, clusters=clusters),
        grid=(heads // PACK_HEADS,),
        in_specs=[head_row(PACK_HEADS, tokens)] + [head_rows(PACK_HEADS)] * 4,
        out_specs=[
            packed_block(PACK_HEADS),
            head_row(PACK_HEADS, tokens),
            head_row(PACK_HEADS, clusters),
        ],
        out_shape=[
            packed_shape,
            jax.ShapeDtypeStruct((heads, 1, tokens), jnp.int32),
            jax.ShapeDtypeStruct((heads, 1, clusters), jnp.int32),
        ],
        scratch_shapes=[scratch(PACK_HEADS)],
        compiler_params=params,
        name="dense_pack_rows",
    )
    attend = pl.pallas_call(
        dense_attention_kernel,
        out_shape=packed_shape,
        scratch_shapes=[
            pltpu.VMEM((steps, SOURCES * OWNED * WIDE), jnp.int32),
            pltpu.VMEM((2, 4 * SOURCES * MESSAGE_ROWS, size), jnp.float32),
            pltpu.VMEM((4, owners * OWNED * WIDE, size), jnp.float32),
        ],
        compiler_params=pltpu.CompilerParams(vmem_limit_bytes=40 * 1024 * 1024),
        name="dense_cluster_attention",
    )
    unpack = pl.pallas_call(
        dense_unpack_kernel,
        grid=(heads // UNPACK_HEADS,),
        in_specs=[head_row(UNPACK_HEADS, tokens), packed_block(UNPACK_HEADS)],
        out_specs=[head_rows(UNPACK_HEADS)] * 4,
        out_shape=[jax.ShapeDtypeStruct((tokens, features), jnp.bfloat16)] * 4,
        scratch_shapes=[scratch(UNPACK_HEADS)],
        compiler_params=params,
        name="dense_unpack_rows",
    )
    return pack, attend, unpack


def exchange(packed, owners):
    moved = lax.all_to_all(
        packed.reshape(owners, -1, packed.shape[1]), "seq", split_axis=0, concat_axis=0, tiled=True
    )
    return moved.reshape(packed.shape)


def body(queries, key_rows, values, grad_out, routes):
    tokens, features = queries.shape
    heads = routes.shape[0]
    owners = lax.axis_size("seq")
    tensors = [
        pltpu.with_memory_space_constraint(array, pltpu.HBM)
        for array in (queries, key_rows, values, grad_out)
    ]
    routes = routes.reshape(heads, 1, tokens)
    pack, attend, unpack = build_dense(tokens, features, heads, owners)
    packed, place, counts = pack(routes, *tensors)
    gathered = lax.all_gather(counts.reshape(heads, -1), "seq")
    loads = jnp.sum(gathered.reshape(owners, heads, -1, OWNED), axis=3)
    fullest = lax.all_gather(jnp.full((8, 128), jnp.max(loads)), "head")
    overflow = jnp.max(fullest) > MESSAGE_ROWS
    own = lax.dynamic_slice_in_dim(
        gathered.reshape(owners, -1), lax.axis_index("seq") * OWNED, OWNED, axis=1
    )
    results = attend(own.reshape(owners // SOURCES, SOURCES * OWNED), exchange(packed, owners))
    returned = exchange(results, owners)

    def padded(place, returned, routes, *tensors):
        pack, attend, unpack = build(tokens, features, heads, owners)
        packed, place = pack(routes, *tensors)
        return tuple(unpack(place, exchange(attend(exchange(packed, owners)), owners)))

    def dense(place, returned, routes, *tensors):
        return tuple(unpack(place, returned))

    return lax.cond(overflow, padded, dense, place, returned, routes, *tensors)


def solution(mesh):
    in_specs = (
        P("seq", "head"),
        P("seq", "head"),
        P("seq", "head"),
        P("seq", "head"),
        P("head", "seq", None),
    )
    out_specs = (P("seq", "head"), P("seq", "head"), P("seq", "head"), P("seq", "head"))
    return jax.shard_map(body, mesh=mesh, in_specs=in_specs, out_specs=out_specs, check_vma=False)
```

```python
import math

import jax
import jax.numpy as jnp
from jax import lax
from jax.experimental import pallas as pl
from jax.experimental.pallas import tpu as pltpu
from jax.sharding import PartitionSpec as P

DEAD_KEY = 256.0
DEAD_TEST = 100.0
PACK_HEADS = 4
ATTEND_HEADS = 2
UNPACK_HEADS = 4
TOKEN_HOPS = 4


def dot_nn(left, right):
    return jnp.dot(left, right, preferred_element_type=jnp.float32)


def dot_nt(left, right):
    return lax.dot_general(left, right, (((1,), (1,)), ((), ())), preferred_element_type=jnp.float32)


def dot_tn(left, right):
    return lax.dot_general(left, right, (((0,), (0,)), ((), ())), preferred_element_type=jnp.float32)


def pack_kernel(routes_ref, q_ref, k_ref, v_ref, g_ref, out_ref, place_ref, scratch, *, owners, slots):
    group, _, tokens = routes_ref.shape
    rows = owners * slots
    size = q_ref.shape[1] // group
    earlier = lax.broadcasted_iota(jnp.int32, (tokens, tokens), 0) < lax.broadcasted_iota(
        jnp.int32, (tokens, tokens), 1
    )
    earlier_low = jnp.where(earlier, 1.0, 0.0).astype(jnp.bfloat16)
    owner_ids = lax.broadcasted_iota(jnp.int32, (owners, tokens), 0)
    row_ids = lax.broadcasted_iota(jnp.int32, (rows, tokens), 0)
    for j in range(group):
        lanes = slice(j * size, (j + 1) * size)
        clusters = routes_ref[j]
        onehot = owner_ids == clusters
        before = dot_nn(jnp.where(onehot, 1.0, 0.0).astype(jnp.bfloat16), earlier_low)
        ranking = jnp.sum(jnp.where(onehot, before, 0.0), axis=0, keepdims=True)
        place = clusters * slots + ranking.astype(jnp.int32)
        place_ref[j] = place
        select = jnp.where(row_ids == place, 1.0, 0.0).astype(jnp.bfloat16)
        query_key = dot_nn(select, jnp.concatenate([q_ref[:, lanes], k_ref[:, lanes]], axis=1))
        value_grad = dot_nn(select, jnp.concatenate([v_ref[:, lanes], g_ref[:, lanes]], axis=1))
        live = dot_nn(select, jnp.ones((tokens, size), jnp.bfloat16))
        scratch[j, pl.ds(0, rows, stride=4), :] = query_key[:, :size]
        scratch[j, pl.ds(1, rows, stride=4), :] = query_key[:, size:] + (1.0 - live) * DEAD_KEY
        scratch[j, pl.ds(2, rows, stride=4), :] = value_grad[:, :size]
        scratch[j, pl.ds(3, rows, stride=4), :] = value_grad[:, size:]
        out_ref[:, lanes] = scratch[j].astype(jnp.bfloat16)


def attention_kernel(in_ref, out_ref, scratch, scratch_out):
    rows = in_ref.shape[0] // 4
    group = scratch.shape[0]
    size = in_ref.shape[1] // group
    scaling = 1.0 / math.sqrt(size)
    first_lane = jnp.where(lax.broadcasted_iota(jnp.int32, (8, size), 1) == 0, 1.0, 0.0)
    first_lane = first_lane.astype(jnp.bfloat16)
    for j in range(group):
        lanes = slice(j * size, (j + 1) * size)
        scratch[j] = in_ref[:, lanes].astype(jnp.float32)
        query, key, value, grad = [
            scratch[j, pl.ds(i, rows, stride=4), :].astype(jnp.bfloat16) for i in range(4)
        ]
        marks = dot_nt(first_lane, key)[0:1]
        scores = dot_nt(query, key) * scaling
        masked = jnp.where(marks < DEAD_TEST, scores, -1e30)
        weights = jnp.exp(masked - jnp.max(masked, axis=1, keepdims=True))
        probability = weights * (1.0 / jnp.sum(weights, axis=1, keepdims=True))
        probability_low = probability.astype(jnp.bfloat16)
        output = dot_nn(probability_low, value).astype(jnp.bfloat16)
        grad_probability = dot_nt(grad, value)
        delta = jnp.sum(
            grad.astype(jnp.float32) * output.astype(jnp.float32), axis=1, keepdims=True
        )
        grad_scores = (probability * (grad_probability - delta)).astype(jnp.bfloat16)
        scratch_out[j, pl.ds(0, rows, stride=4), :] = output.astype(jnp.float32)
        scratch_out[j, pl.ds(1, rows, stride=4), :] = dot_nn(grad_scores, key) * scaling
        scratch_out[j, pl.ds(2, rows, stride=4), :] = dot_tn(grad_scores, query) * scaling
        scratch_out[j, pl.ds(3, rows, stride=4), :] = dot_tn(probability_low, grad)
        out_ref[:, lanes] = scratch_out[j].astype(jnp.bfloat16)


def unpack_kernel(place_ref, in_ref, token_ref, o_ref, dq_ref, dk_ref, dv_ref, scratch):
    rows = in_ref.shape[0] // 4
    group, _, tokens = place_ref.shape
    size = o_ref.shape[1] // group
    row_ids = lax.broadcasted_iota(jnp.int32, (rows, tokens), 0)
    for j in range(group):
        lanes = slice(j * size, (j + 1) * size)
        scratch[j] = in_ref[:, lanes].astype(jnp.float32)
        select = jnp.where(row_ids == place_ref[j], 1.0, 0.0).astype(jnp.bfloat16)
        parts = [scratch[j, pl.ds(i, rows, stride=4), :].astype(jnp.bfloat16) for i in range(4)]
        first = dot_tn(select, jnp.concatenate(parts[:2], axis=1)).astype(jnp.bfloat16)
        second = dot_tn(select, jnp.concatenate(parts[2:], axis=1)).astype(jnp.bfloat16)
        o_ref[:, lanes] = first[:, :size]
        dq_ref[:, lanes] = first[:, size:]
        dk_ref[:, lanes] = second[:, :size]
        dv_ref[:, lanes] = second[:, size:]


def build(tokens, features, heads, owners):
    size = features // heads
    slots = 3 * tokens // (2 * owners)
    rows = owners * slots
    params = pltpu.CompilerParams(
        dimension_semantics=("arbitrary",), vmem_limit_bytes=56 * 1024 * 1024
    )
    packed_shape = jax.ShapeDtypeStruct((4 * rows, features), jnp.bfloat16)

    def head_rows(group):
        return pl.BlockSpec((tokens, group * size), lambda h: (0, h))

    def head_row(group):
        return pl.BlockSpec((group, 1, tokens), lambda h: (h, 0, 0))

    def packed_block(group):
        return pl.BlockSpec((4 * rows, group * size), lambda h: (0, h))

    def scratch(group):
        return pltpu.VMEM((group, 4 * rows, size), jnp.float32)

    pack = pl.pallas_call(
        lambda *refs: pack_kernel(*refs, owners=owners, slots=slots),
        grid=(heads // PACK_HEADS,),
        in_specs=[head_row(PACK_HEADS)] + [head_rows(PACK_HEADS)] * 4,
        out_specs=[packed_block(PACK_HEADS), head_row(PACK_HEADS)],
        out_shape=[packed_shape, jax.ShapeDtypeStruct((heads, 1, tokens), jnp.int32)],
        scratch_shapes=[scratch(PACK_HEADS)],
        compiler_params=params,
        name="pack_rows",
    )
    attend = pl.pallas_call(
        attention_kernel,
        grid=(heads // ATTEND_HEADS,),
        in_specs=[packed_block(ATTEND_HEADS)],
        out_specs=packed_block(ATTEND_HEADS),
        out_shape=packed_shape,
        scratch_shapes=[scratch(ATTEND_HEADS)] * 2,
        compiler_params=params,
        name="cluster_attention",
    )
    unpack = pl.pallas_call(
        unpack_kernel,
        grid=(heads // UNPACK_HEADS,),
        in_specs=[
            head_row(UNPACK_HEADS),
            packed_block(UNPACK_HEADS),
            pl.BlockSpec(memory_space=pl.ANY),
        ],
        out_specs=[head_rows(UNPACK_HEADS)] * 4,
        out_shape=[jax.ShapeDtypeStruct((tokens, features), jnp.bfloat16)] * 4,
        scratch_shapes=[scratch(UNPACK_HEADS)],
        compiler_params=params,
        name="unpack_rows",
    )
    return pack, attend, unpack


def body(queries, key_rows, values, grad_out, routes):
    tokens, features = queries.shape
    heads = routes.shape[0]
    owners = lax.axis_size("seq")
    pack, attend, unpack = build(tokens, features, heads, owners)

    def exchange(packed):
        moved = lax.all_to_all(
            packed.reshape(owners, -1, features), "seq", split_axis=0, concat_axis=0, tiled=True
        )
        return moved.reshape(packed.shape)

    def in_hbm(array):
        return pltpu.with_memory_space_constraint(array, pltpu.HBM)

    packed, place = pack(
        routes.reshape(heads, 1, tokens),
        in_hbm(queries),
        in_hbm(key_rows),
        in_hbm(values),
        in_hbm(grad_out),
    )
    token = place[:, 0, :128]
    groups = lax.axis_size("head")
    turns = [
        (s * groups + h, (s + owners // 2 + 8) % owners * groups + h)
        for s in range(owners)
        for h in range(1, groups, 2)
    ]
    for _ in range(TOKEN_HOPS):
        token = jnp.maximum(token, lax.ppermute(token, ("seq", "head"), turns))
    packed, token = lax.optimization_barrier((packed, token))
    results = attend(exchange(packed))
    return tuple(unpack(place, exchange(results), token))


def solution(mesh):
    in_specs = (
        P("seq", "head"),
        P("seq", "head"),
        P("seq", "head"),
        P("seq", "head"),
        P("head", "seq", None),
    )
    out_specs = (P("seq", "head"), P("seq", "head"), P("seq", "head"), P("seq", "head"))
    return jax.shard_map(body, mesh=mesh, in_specs=in_specs, out_specs=out_specs, check_vma=False)
```

```python
import math

import jax
import jax.numpy as jnp
from jax import lax
from jax.experimental import pallas as pl
from jax.experimental.pallas import tpu as pltpu
from jax.sharding import PartitionSpec as P

DEAD_KEY = 256.0
DEAD_TEST = 100.0
MESSAGE_ROWS = 44
OWNED = 8
WIDE = 8
SOURCES = 4
PACK_HEADS = 4
ATTEND_HEADS = 2
UNPACK_HEADS = 4
TOKEN_HOPS = 3


def dot_nn(left, right):
    return jnp.dot(left, right, preferred_element_type=jnp.float32)


def dot_nt(left, right):
    return lax.dot_general(left, right, (((1,), (1,)), ((), ())), preferred_element_type=jnp.float32)


def dot_tn(left, right):
    return lax.dot_general(left, right, (((0,), (0,)), ((), ())), preferred_element_type=jnp.float32)


def pack_kernel(routes_ref, q_ref, k_ref, v_ref, g_ref, out_ref, place_ref, scratch, *, owners, slots):
    group, _, tokens = routes_ref.shape
    rows = owners * slots
    size = q_ref.shape[1] // group
    earlier = lax.broadcasted_iota(jnp.int32, (tokens, tokens), 0) < lax.broadcasted_iota(
        jnp.int32, (tokens, tokens), 1
    )
    earlier_low = jnp.where(earlier, 1.0, 0.0).astype(jnp.bfloat16)
    owner_ids = lax.broadcasted_iota(jnp.int32, (owners, tokens), 0)
    row_ids = lax.broadcasted_iota(jnp.int32, (rows, tokens), 0)
    for j in range(group):
        lanes = slice(j * size, (j + 1) * size)
        clusters = routes_ref[j]
        onehot = owner_ids == clusters
        before = dot_nn(jnp.where(onehot, 1.0, 0.0).astype(jnp.bfloat16), earlier_low)
        ranking = jnp.sum(jnp.where(onehot, before, 0.0), axis=0, keepdims=True)
        place = clusters * slots + ranking.astype(jnp.int32)
        place_ref[j] = place
        select = jnp.where(row_ids == place, 1.0, 0.0).astype(jnp.bfloat16)
        query_key = dot_nn(select, jnp.concatenate([q_ref[:, lanes], k_ref[:, lanes]], axis=1))
        value_grad = dot_nn(select, jnp.concatenate([v_ref[:, lanes], g_ref[:, lanes]], axis=1))
        live = dot_nn(select, jnp.ones((tokens, size), jnp.bfloat16))
        scratch[j, pl.ds(0, rows, stride=4), :] = query_key[:, :size]
        scratch[j, pl.ds(1, rows, stride=4), :] = query_key[:, size:] + (1.0 - live) * DEAD_KEY
        scratch[j, pl.ds(2, rows, stride=4), :] = value_grad[:, :size]
        scratch[j, pl.ds(3, rows, stride=4), :] = value_grad[:, size:]
        out_ref[:, lanes] = scratch[j].astype(jnp.bfloat16)


def attend_cluster(query, key, value, grad, keep):
    size = query.shape[1]
    scaling = 1.0 / math.sqrt(size)
    scores = dot_nt(query, key) * scaling
    masked = jnp.where(keep, scores, -1e30)
    weights = jnp.exp(masked - jnp.max(masked, axis=1, keepdims=True))
    probability = weights * (1.0 / jnp.sum(weights, axis=1, keepdims=True))
    probability_low = probability.astype(jnp.bfloat16)
    output = dot_nn(probability_low, value).astype(jnp.bfloat16).astype(jnp.float32)
    grad_probability = dot_nt(grad, value)
    delta = jnp.sum(grad.astype(jnp.float32) * output, axis=1, keepdims=True)
    grad_scores = (probability * (grad_probability - delta)).astype(jnp.bfloat16)
    return (
        output,
        dot_nn(grad_scores, key) * scaling,
        dot_tn(grad_scores, query) * scaling,
        dot_tn(probability_low, grad),
    )


def attention_kernel(in_ref, out_ref, scratch, scratch_out):
    rows = in_ref.shape[0] // 4
    group = scratch.shape[0]
    size = in_ref.shape[1] // group
    for j in range(group):
        lanes = slice(j * size, (j + 1) * size)
        scratch[j] = in_ref[:, lanes].astype(jnp.float32)
        tensors = [scratch[j, pl.ds(i, rows, stride=4), :].astype(jnp.bfloat16) for i in range(4)]
        first_lane = jnp.where(lax.broadcasted_iota(jnp.int32, (8, size), 1) == 0, 1.0, 0.0)
        keep = dot_nt(first_lane.astype(jnp.bfloat16), tensors[1])[0:1] < DEAD_TEST
        for i, result in enumerate(attend_cluster(*tensors, keep)):
            scratch_out[j, pl.ds(i, rows, stride=4), :] = result
        out_ref[:, lanes] = scratch_out[j].astype(jnp.bfloat16)


def unpack_kernel(place_ref, in_ref, o_ref, dq_ref, dk_ref, dv_ref, scratch):
    rows = in_ref.shape[0] // 4
    group, _, tokens = place_ref.shape
    size = o_ref.shape[1] // group
    row_ids = lax.broadcasted_iota(jnp.int32, (rows, tokens), 0)
    for j in range(group):
        lanes = slice(j * size, (j + 1) * size)
        scratch[j] = in_ref[:, lanes].astype(jnp.float32)
        select = jnp.where(row_ids == place_ref[j], 1.0, 0.0).astype(jnp.bfloat16)
        parts = [scratch[j, pl.ds(i, rows, stride=4), :].astype(jnp.bfloat16) for i in range(4)]
        first = dot_tn(select, jnp.concatenate(parts[:2], axis=1)).astype(jnp.bfloat16)
        second = dot_tn(select, jnp.concatenate(parts[2:], axis=1)).astype(jnp.bfloat16)
        o_ref[:, lanes] = first[:, :size]
        dq_ref[:, lanes] = first[:, size:]
        dk_ref[:, lanes] = second[:, :size]
        dv_ref[:, lanes] = second[:, size:]


def dense_pack_kernel(
    routes_ref, q_ref, k_ref, v_ref, g_ref, out_ref, place_ref, scratch, *, clusters
):
    group, _, tokens = routes_ref.shape
    rows = scratch.shape[1] // 4
    size = q_ref.shape[1] // group
    octets = clusters // OWNED
    earlier = lax.broadcasted_iota(jnp.int32, (tokens, tokens), 0) < lax.broadcasted_iota(
        jnp.int32, (tokens, tokens), 1
    )
    earlier_low = jnp.where(earlier, 1.0, 0.0).astype(jnp.bfloat16)
    this = lax.broadcasted_iota(jnp.int32, (clusters, clusters), 0)
    other = lax.broadcasted_iota(jnp.int32, (clusters, clusters), 1)
    lower = jnp.logical_and(other < this, other // OWNED == this // OWNED)
    lower_low = jnp.where(lower, 1.0, 0.0).astype(jnp.bfloat16)
    all_tokens = jnp.ones((tokens, tokens), jnp.bfloat16)
    cluster_ids = lax.broadcasted_iota(jnp.int32, (clusters, tokens), 0)
    row_ids = lax.broadcasted_iota(jnp.int32, (rows, tokens), 0)
    in_octet = lax.broadcasted_iota(jnp.int32, (octets, clusters), 1) // OWNED == (
        lax.broadcasted_iota(jnp.int32, (octets, clusters), 0)
    )
    to_lane = lax.broadcasted_iota(jnp.int32, (clusters, size), 0) % OWNED == (
        lax.broadcasted_iota(jnp.int32, (clusters, size), 1)
    )
    to_lane_low = jnp.where(to_lane, 1.0, 0.0).astype(jnp.bfloat16)
    for j in range(group):
        lanes = slice(j * size, (j + 1) * size)
        route = routes_ref[j]
        onehot = cluster_ids == route
        onehot_low = jnp.where(onehot, 1.0, 0.0).astype(jnp.bfloat16)
        counts = dot_nt(all_tokens[:octets], onehot_low)
        counts = jnp.where(in_octet, counts, 0.0)
        in_lower = dot_nn(lower_low, onehot_low).astype(jnp.bfloat16)
        before = dot_nn(onehot_low, earlier_low) + dot_nn(in_lower, all_tokens)
        ranking = jnp.sum(jnp.where(onehot, before, 0.0), axis=0, keepdims=True)
        place = route // OWNED * MESSAGE_ROWS + 1 + ranking.astype(jnp.int32)
        place_ref[j] = place
        select = jnp.where(row_ids == place, 1.0, 0.0).astype(jnp.bfloat16)
        query_key = dot_nn(select, jnp.concatenate([q_ref[:, lanes], k_ref[:, lanes]], axis=1))
        value_grad = dot_nn(select, jnp.concatenate([v_ref[:, lanes], g_ref[:, lanes]], axis=1))
        scratch[j, pl.ds(0, rows, stride=4), :] = query_key[:, :size]
        scratch[j, pl.ds(1, rows, stride=4), :] = query_key[:, size:]
        scratch[j, pl.ds(2, rows, stride=4), :] = value_grad[:, :size]
        scratch[j, pl.ds(3, rows, stride=4), :] = value_grad[:, size:]
        scratch[j, pl.ds(0, octets, stride=4 * MESSAGE_ROWS), :] = dot_nn(
            counts.astype(jnp.bfloat16), to_lane_low
        )
        out_ref[j * 4 * rows : (j + 1) * 4 * rows, :] = scratch[j].astype(jnp.bfloat16)


def dense_attention_kernel(
    in_ref, token_ref, out_ref, target_ref, stage, wide_ref, *, slots
):
    size = in_ref.shape[1]
    count = SOURCES * MESSAGE_ROWS
    wide = SOURCES * OWNED * WIDE
    sources = in_ref.shape[0] // (4 * MESSAGE_ROWS)
    steps = sources // SOURCES
    for s in range(sources):
        head_rows = in_ref[s * 4 * MESSAGE_ROWS : s * 4 * MESSAGE_ROWS + 16, :]
        stage[0, s : s + 1, :] = head_rows.astype(jnp.float32)[0:1]
    counts = stage[0, 0:sources, :]
    counts_low = counts.astype(jnp.bfloat16)
    most = jnp.max(jnp.sum(counts, axis=1, keepdims=True), axis=0, keepdims=True)
    overflow = jnp.broadcast_to(jnp.where(most > MESSAGE_ROWS - 1, 1.0, 0.0), (SOURCES, size))
    lane = lax.broadcasted_iota(jnp.int32, (size, wide), 1)
    lane_cluster = lane // WIDE % OWNED
    cluster = lax.broadcasted_iota(jnp.int32, (size, wide), 0)
    same = jnp.where(lane_cluster == cluster, 1.0, 0.0).astype(jnp.bfloat16)
    ahead = jnp.where(cluster < lane_cluster, 1.0, 0.0).astype(jnp.bfloat16)
    lane = lax.broadcasted_iota(jnp.int32, (sources, wide), 1)
    source = lax.broadcasted_iota(jnp.int32, (sources, wide), 0)
    slot = lane % WIDE
    spread = dot_nn(counts_low, same).astype(jnp.int32)
    target = dot_nn(counts_low, ahead).astype(jnp.int32) + slot + 1 + source % SOURCES * MESSAGE_ROWS
    live = jnp.logical_and(slot < spread, lane // (OWNED * WIDE) == source % SOURCES)
    steps_of = lax.broadcasted_iota(jnp.int32, (steps, sources), 1) // SOURCES == (
        lax.broadcasted_iota(jnp.int32, (steps, sources), 0)
    )
    target_ref[...] = dot_nn(
        jnp.where(steps_of, 1.0, 0.0).astype(jnp.bfloat16),
        jnp.where(live, target, 0).astype(jnp.float32).astype(jnp.bfloat16),
    ).astype(jnp.int32)
    slot_lane = lax.broadcasted_iota(jnp.int32, (sources, slots * sources), 1)
    repeat = lax.broadcasted_iota(jnp.int32, (sources, slots * sources), 0) == slot_lane % sources
    repeated = lax.dot_general(
        counts_low,
        jnp.where(repeat, 1.0, 0.0).astype(jnp.bfloat16),
        (((0,), (0,)), ((), ())),
        preferred_element_type=jnp.float32,
    )[:OWNED].astype(jnp.int32)
    keep = repeated > lax.broadcasted_iota(jnp.int32, (OWNED, slots * sources), 1) // sources
    row_ids = lax.broadcasted_iota(jnp.int32, (count, wide), 0)

    def selection(step):
        target = target_ref[pl.ds(step, 1), :]
        select = jnp.logical_and(row_ids == target, target > 0)
        return jnp.where(select, 1.0, 0.0).astype(jnp.bfloat16)

    def expand(pass_id, carry):
        for u in range(stage.shape[0]):
            step = pass_id * stage.shape[0] + u
            stage[u] = in_ref[pl.ds(step * 4 * count, 4 * count), :].astype(jnp.float32)
            parts = [stage[u, pl.ds(i, count, stride=4), :].astype(jnp.bfloat16) for i in range(4)]
            select = selection(step)
            into = pl.ds(step * wide, wide)
            query_key = dot_tn(select, jnp.concatenate(parts[:2], axis=1))
            value_grad = dot_tn(select, jnp.concatenate(parts[2:], axis=1))
            wide_ref[0, into, :] = query_key[:, :size]
            wide_ref[1, into, :] = query_key[:, size:]
            wide_ref[2, into, :] = value_grad[:, :size]
            wide_ref[3, into, :] = value_grad[:, size:]
        return carry

    def compact(pass_id, carry):
        for u in range(stage.shape[0]):
            step = pass_id * stage.shape[0] + u
            select = selection(step)
            parts = [
                wide_ref[i, pl.ds(step * wide, wide), :].astype(jnp.bfloat16) for i in range(4)
            ]
            first = dot_nn(select, jnp.concatenate(parts[:2], axis=1))
            second = dot_nn(select, jnp.concatenate(parts[2:], axis=1))
            stage[u, pl.ds(0, count, stride=4), :] = first[:, :size]
            stage[u, pl.ds(1, count, stride=4), :] = first[:, size:]
            stage[u, pl.ds(2, count, stride=4), :] = second[:, :size]
            stage[u, pl.ds(3, count, stride=4), :] = second[:, size:]
            stage[u, pl.ds(0, SOURCES, stride=4 * MESSAGE_ROWS), :] = overflow
            out_ref[pl.ds(step * 4 * count, 4 * count), :] = stage[u].astype(jnp.bfloat16)
        return carry

    lax.fori_loop(0, steps // stage.shape[0], expand, 0)
    for c in range(OWNED):
        spots = [pl.ds(c * WIDE + s, sources, stride=OWNED * WIDE) for s in range(slots)]
        tensors = [
            jnp.concatenate([wide_ref[i, spot, :] for spot in spots], axis=0).astype(jnp.bfloat16)
            for i in range(4)
        ]
        for i, result in enumerate(attend_cluster(*tensors, keep[c : c + 1])):
            for s, spot in enumerate(spots):
                wide_ref[i, spot, :] = result[s * sources : (s + 1) * sources]
    lax.fori_loop(0, steps // stage.shape[0], compact, 0)


def dense_unpack_kernel(place_ref, in_ref, o_ref, dq_ref, dk_ref, dv_ref, scratch):
    rows = scratch.shape[1] // 4
    group, _, tokens = place_ref.shape
    size = o_ref.shape[1] // group
    row_ids = lax.broadcasted_iota(jnp.int32, (rows, tokens), 0)
    for j in range(group):
        lanes = slice(j * size, (j + 1) * size)
        scratch[j] = in_ref[j * 4 * rows : (j + 1) * 4 * rows, :].astype(jnp.float32)
        select = jnp.where(row_ids == place_ref[j], 1.0, 0.0).astype(jnp.bfloat16)
        parts = [scratch[j, pl.ds(i, rows, stride=4), :].astype(jnp.bfloat16) for i in range(4)]
        first = dot_tn(select, jnp.concatenate(parts[:2], axis=1)).astype(jnp.bfloat16)
        second = dot_tn(select, jnp.concatenate(parts[2:], axis=1)).astype(jnp.bfloat16)
        o_ref[:, lanes] = first[:, :size]
        dq_ref[:, lanes] = first[:, size:]
        dk_ref[:, lanes] = second[:, :size]
        dv_ref[:, lanes] = second[:, size:]


def build(tokens, features, heads, owners):
    size = features // heads
    slots = 3 * tokens // (2 * owners)
    rows = owners * slots
    params = pltpu.CompilerParams(
        dimension_semantics=("arbitrary",), vmem_limit_bytes=40 * 1024 * 1024
    )
    packed_shape = jax.ShapeDtypeStruct((4 * rows, features), jnp.bfloat16)

    def head_rows(group):
        return pl.BlockSpec((tokens, group * size), lambda h: (0, h))

    def head_row(group):
        return pl.BlockSpec((group, 1, tokens), lambda h: (h, 0, 0))

    def packed_block(group):
        return pl.BlockSpec((4 * rows, group * size), lambda h: (0, h))

    def scratch(group):
        return pltpu.VMEM((group, 4 * rows, size), jnp.float32)

    pack = pl.pallas_call(
        lambda *refs: pack_kernel(*refs, owners=owners, slots=slots),
        grid=(heads // PACK_HEADS,),
        in_specs=[head_row(PACK_HEADS)] + [head_rows(PACK_HEADS)] * 4,
        out_specs=[packed_block(PACK_HEADS), head_row(PACK_HEADS)],
        out_shape=[packed_shape, jax.ShapeDtypeStruct((heads, 1, tokens), jnp.int32)],
        scratch_shapes=[scratch(PACK_HEADS)],
        compiler_params=params,
        name="pack_rows",
    )
    attend = pl.pallas_call(
        attention_kernel,
        grid=(heads // ATTEND_HEADS,),
        in_specs=[packed_block(ATTEND_HEADS)],
        out_specs=packed_block(ATTEND_HEADS),
        out_shape=packed_shape,
        scratch_shapes=[scratch(ATTEND_HEADS)] * 2,
        compiler_params=params,
        name="cluster_attention",
    )
    unpack = pl.pallas_call(
        unpack_kernel,
        grid=(heads // UNPACK_HEADS,),
        in_specs=[head_row(UNPACK_HEADS), packed_block(UNPACK_HEADS)],
        out_specs=[head_rows(UNPACK_HEADS)] * 4,
        out_shape=[jax.ShapeDtypeStruct((tokens, features), jnp.bfloat16)] * 4,
        scratch_shapes=[scratch(UNPACK_HEADS)],
        compiler_params=params,
        name="unpack_rows",
    )
    return pack, attend, unpack


def build_dense(tokens, features, heads, owners):
    size = features // heads
    clusters = heads * OWNED
    rows = OWNED * MESSAGE_ROWS
    slots = 3 * tokens // (2 * owners)
    params = pltpu.CompilerParams(
        dimension_semantics=("arbitrary",), vmem_limit_bytes=60 * 1024 * 1024
    )
    packed_shape = jax.ShapeDtypeStruct((heads * 4 * rows, size), jnp.bfloat16)

    def head_rows(group):
        return pl.BlockSpec((tokens, group * size), lambda h: (0, h))

    def head_row(group, length):
        return pl.BlockSpec((group, 1, length), lambda h: (h, 0, 0))

    def packed_block(group):
        return pl.BlockSpec((group * 4 * rows, size), lambda h: (h, 0))

    def scratch(group):
        return pltpu.VMEM((group, 4 * rows, size), jnp.float32)

    pack = pl.pallas_call(
        lambda *refs: dense_pack_kernel(*refs, clusters=clusters),
        grid=(heads // PACK_HEADS,),
        in_specs=[head_row(PACK_HEADS, tokens)] + [head_rows(PACK_HEADS)] * 4,
        out_specs=[
            packed_block(PACK_HEADS),
            head_row(PACK_HEADS, tokens),
        ],
        out_shape=[
            packed_shape,
            jax.ShapeDtypeStruct((heads, 1, tokens), jnp.int32),
        ],
        scratch_shapes=[scratch(PACK_HEADS)],
        compiler_params=params,
        name="dense_pack_rows",
    )
    attend = pl.pallas_call(
        lambda *refs: dense_attention_kernel(*refs, slots=slots),
        in_specs=[pl.BlockSpec(memory_space=pltpu.VMEM), pl.BlockSpec(memory_space=pl.ANY)],
        out_shape=packed_shape,
        scratch_shapes=[
            pltpu.VMEM((owners // SOURCES, SOURCES * OWNED * WIDE), jnp.int32),
            pltpu.VMEM((2, 4 * SOURCES * MESSAGE_ROWS, size), jnp.float32),
            pltpu.VMEM((4, owners * OWNED * WIDE, size), jnp.float32),
        ],
        compiler_params=pltpu.CompilerParams(vmem_limit_bytes=40 * 1024 * 1024),
        name="dense_cluster_attention",
    )
    unpack = pl.pallas_call(
        dense_unpack_kernel,
        grid=(heads // UNPACK_HEADS,),
        in_specs=[head_row(UNPACK_HEADS, tokens), packed_block(UNPACK_HEADS)],
        out_specs=[head_rows(UNPACK_HEADS)] * 4,
        out_shape=[jax.ShapeDtypeStruct((tokens, features), jnp.bfloat16)] * 4,
        scratch_shapes=[scratch(UNPACK_HEADS)],
        compiler_params=params,
        name="dense_unpack_rows",
    )
    return pack, attend, unpack


def exchange(packed, owners):
    moved = lax.all_to_all(
        packed.reshape(owners, -1, packed.shape[1]), "seq", split_axis=0, concat_axis=0, tiled=True
    )
    return moved.reshape(packed.shape)


def body(queries, key_rows, values, grad_out, routes):
    tokens, features = queries.shape
    heads = routes.shape[0]
    owners = lax.axis_size("seq")
    tensors = [
        pltpu.with_memory_space_constraint(array, pltpu.HBM)
        for array in (queries, key_rows, values, grad_out)
    ]
    routes = routes.reshape(heads, 1, tokens)
    pack, attend, unpack = build_dense(tokens, features, heads, owners)
    packed, place = pack(routes, *tensors)
    token = place[:, 0, :128]
    groups = lax.axis_size("head")
    turns = [
        (s * groups + h, (s + owners // 2 + 8) % owners * groups + h)
        for s in range(owners)
        for h in range(1, groups, 2)
    ]
    for _ in range(TOKEN_HOPS):
        token = jnp.maximum(token, lax.ppermute(token, ("seq", "head"), turns))
    packed, token = lax.optimization_barrier((packed, token))
    returned = exchange(attend(exchange(packed, owners), token), owners)
    overflow = jnp.max(returned.reshape(owners, -1, returned.shape[1])[:, 0, 0]) > 0.5

    def padded(place, returned, routes, *tensors):
        pack, attend, unpack = build(tokens, features, heads, owners)
        packed, place = pack(routes, *tensors)
        return tuple(unpack(place, exchange(attend(exchange(packed, owners)), owners)))

    def dense(place, returned, routes, *tensors):
        return tuple(unpack(place, returned))

    return lax.cond(overflow, padded, dense, place, returned, routes, *tensors)


def solution(mesh):
    in_specs = (
        P("seq", "head"),
        P("seq", "head"),
        P("seq", "head"),
        P("seq", "head"),
        P("head", "seq", None),
    )
    out_specs = (P("seq", "head"), P("seq", "head"), P("seq", "head"), P("seq", "head"))
    return jax.shard_map(body, mesh=mesh, in_specs=in_specs, out_specs=out_specs, check_vma=False)
```

```python
import math

import jax
import jax.numpy as jnp
from jax import lax
from jax.experimental import pallas as pl
from jax.experimental.pallas import tpu as pltpu
from jax.sharding import PartitionSpec as P

DEAD_KEY = 256.0
DEAD_TEST = 100.0
MESSAGE_ROWS = 44
OWNED = 8
WIDE = 8
SOURCES = 4
PACK_HEADS = 4
ATTEND_HEADS = 2
UNPACK_HEADS = 4
TOKEN_HOPS = 2


def dot_nn(left, right):
    return jnp.dot(left, right, preferred_element_type=jnp.float32)


def dot_nt(left, right):
    return lax.dot_general(left, right, (((1,), (1,)), ((), ())), preferred_element_type=jnp.float32)


def dot_tn(left, right):
    return lax.dot_general(left, right, (((0,), (0,)), ((), ())), preferred_element_type=jnp.float32)


def pack_kernel(routes_ref, q_ref, k_ref, v_ref, g_ref, out_ref, place_ref, scratch, *, owners, slots):
    group, _, tokens = routes_ref.shape
    rows = owners * slots
    size = q_ref.shape[1] // group
    earlier = lax.broadcasted_iota(jnp.int32, (tokens, tokens), 0) < lax.broadcasted_iota(
        jnp.int32, (tokens, tokens), 1
    )
    earlier_low = jnp.where(earlier, 1.0, 0.0).astype(jnp.bfloat16)
    owner_ids = lax.broadcasted_iota(jnp.int32, (owners, tokens), 0)
    row_ids = lax.broadcasted_iota(jnp.int32, (rows, tokens), 0)
    for j in range(group):
        lanes = slice(j * size, (j + 1) * size)
        clusters = routes_ref[j]
        onehot = owner_ids == clusters
        before = dot_nn(jnp.where(onehot, 1.0, 0.0).astype(jnp.bfloat16), earlier_low)
        ranking = jnp.sum(jnp.where(onehot, before, 0.0), axis=0, keepdims=True)
        place = clusters * slots + ranking.astype(jnp.int32)
        place_ref[j] = place
        select = jnp.where(row_ids == place, 1.0, 0.0).astype(jnp.bfloat16)
        query_key = dot_nn(select, jnp.concatenate([q_ref[:, lanes], k_ref[:, lanes]], axis=1))
        value_grad = dot_nn(select, jnp.concatenate([v_ref[:, lanes], g_ref[:, lanes]], axis=1))
        live = dot_nn(select, jnp.ones((tokens, size), jnp.bfloat16))
        scratch[j, pl.ds(0, rows, stride=4), :] = query_key[:, :size]
        scratch[j, pl.ds(1, rows, stride=4), :] = query_key[:, size:] + (1.0 - live) * DEAD_KEY
        scratch[j, pl.ds(2, rows, stride=4), :] = value_grad[:, :size]
        scratch[j, pl.ds(3, rows, stride=4), :] = value_grad[:, size:]
        out_ref[:, lanes] = scratch[j].astype(jnp.bfloat16)


def attend_cluster(query, key, value, grad, keep):
    size = query.shape[1]
    scaling = 1.0 / math.sqrt(size)
    scores = dot_nt(query, key) * scaling
    masked = jnp.where(keep, scores, -1e30)
    weights = jnp.exp(masked - jnp.max(masked, axis=1, keepdims=True))
    probability = weights * (1.0 / jnp.sum(weights, axis=1, keepdims=True))
    probability_low = probability.astype(jnp.bfloat16)
    output = dot_nn(probability_low, value).astype(jnp.bfloat16).astype(jnp.float32)
    grad_probability = dot_nt(grad, value)
    delta = jnp.sum(grad.astype(jnp.float32) * output, axis=1, keepdims=True)
    grad_scores = (probability * (grad_probability - delta)).astype(jnp.bfloat16)
    return (
        output,
        dot_nn(grad_scores, key) * scaling,
        dot_tn(grad_scores, query) * scaling,
        dot_tn(probability_low, grad),
    )


def attention_kernel(in_ref, out_ref, scratch, scratch_out):
    rows = in_ref.shape[0] // 4
    group = scratch.shape[0]
    size = in_ref.shape[1] // group
    for j in range(group):
        lanes = slice(j * size, (j + 1) * size)
        scratch[j] = in_ref[:, lanes].astype(jnp.float32)
        tensors = [scratch[j, pl.ds(i, rows, stride=4), :].astype(jnp.bfloat16) for i in range(4)]
        first_lane = jnp.where(lax.broadcasted_iota(jnp.int32, (8, size), 1) == 0, 1.0, 0.0)
        keep = dot_nt(first_lane.astype(jnp.bfloat16), tensors[1])[0:1] < DEAD_TEST
        for i, result in enumerate(attend_cluster(*tensors, keep)):
            scratch_out[j, pl.ds(i, rows, stride=4), :] = result
        out_ref[:, lanes] = scratch_out[j].astype(jnp.bfloat16)


def unpack_kernel(place_ref, in_ref, o_ref, dq_ref, dk_ref, dv_ref, scratch):
    rows = in_ref.shape[0] // 4
    group, _, tokens = place_ref.shape
    size = o_ref.shape[1] // group
    row_ids = lax.broadcasted_iota(jnp.int32, (rows, tokens), 0)
    for j in range(group):
        lanes = slice(j * size, (j + 1) * size)
        scratch[j] = in_ref[:, lanes].astype(jnp.float32)
        select = jnp.where(row_ids == place_ref[j], 1.0, 0.0).astype(jnp.bfloat16)
        parts = [scratch[j, pl.ds(i, rows, stride=4), :].astype(jnp.bfloat16) for i in range(4)]
        first = dot_tn(select, jnp.concatenate(parts[:2], axis=1)).astype(jnp.bfloat16)
        second = dot_tn(select, jnp.concatenate(parts[2:], axis=1)).astype(jnp.bfloat16)
        o_ref[:, lanes] = first[:, :size]
        dq_ref[:, lanes] = first[:, size:]
        dk_ref[:, lanes] = second[:, :size]
        dv_ref[:, lanes] = second[:, size:]


def dense_pack_kernel(
    routes_ref, q_ref, k_ref, v_ref, g_ref, out_ref, place_ref, scratch, *, clusters
):
    group, _, tokens = routes_ref.shape
    rows = scratch.shape[1] // 4
    size = q_ref.shape[1] // group
    octets = clusters // OWNED
    earlier = lax.broadcasted_iota(jnp.int32, (tokens, tokens), 0) < lax.broadcasted_iota(
        jnp.int32, (tokens, tokens), 1
    )
    earlier_low = jnp.where(earlier, 1.0, 0.0).astype(jnp.bfloat16)
    this = lax.broadcasted_iota(jnp.int32, (clusters, clusters), 0)
    other = lax.broadcasted_iota(jnp.int32, (clusters, clusters), 1)
    lower = jnp.logical_and(other < this, other // OWNED == this // OWNED)
    lower_low = jnp.where(lower, 1.0, 0.0).astype(jnp.bfloat16)
    all_tokens = jnp.ones((tokens, tokens), jnp.bfloat16)
    cluster_ids = lax.broadcasted_iota(jnp.int32, (clusters, tokens), 0)
    row_ids = lax.broadcasted_iota(jnp.int32, (rows, tokens), 0)
    in_octet = lax.broadcasted_iota(jnp.int32, (octets, clusters), 1) // OWNED == (
        lax.broadcasted_iota(jnp.int32, (octets, clusters), 0)
    )
    to_lane = lax.broadcasted_iota(jnp.int32, (clusters, size), 0) % OWNED == (
        lax.broadcasted_iota(jnp.int32, (clusters, size), 1)
    )
    to_lane_low = jnp.where(to_lane, 1.0, 0.0).astype(jnp.bfloat16)
    for j in range(group):
        lanes = slice(j * size, (j + 1) * size)
        route = routes_ref[j]
        onehot = cluster_ids == route
        onehot_low = jnp.where(onehot, 1.0, 0.0).astype(jnp.bfloat16)
        counts = dot_nt(all_tokens[:octets], onehot_low)
        counts = jnp.where(in_octet, counts, 0.0)
        in_lower = dot_nn(lower_low, onehot_low).astype(jnp.bfloat16)
        before = dot_nn(onehot_low, earlier_low) + dot_nn(in_lower, all_tokens)
        ranking = jnp.sum(jnp.where(onehot, before, 0.0), axis=0, keepdims=True)
        place = route // OWNED * MESSAGE_ROWS + 1 + ranking.astype(jnp.int32)
        place_ref[j] = place
        select = jnp.where(row_ids == place, 1.0, 0.0).astype(jnp.bfloat16)
        query_key = dot_nn(select, jnp.concatenate([q_ref[:, lanes], k_ref[:, lanes]], axis=1))
        value_grad = dot_nn(select, jnp.concatenate([v_ref[:, lanes], g_ref[:, lanes]], axis=1))
        scratch[j, pl.ds(0, rows, stride=4), :] = query_key[:, :size]
        scratch[j, pl.ds(1, rows, stride=4), :] = query_key[:, size:]
        scratch[j, pl.ds(2, rows, stride=4), :] = value_grad[:, :size]
        scratch[j, pl.ds(3, rows, stride=4), :] = value_grad[:, size:]
        scratch[j, pl.ds(0, octets, stride=4 * MESSAGE_ROWS), :] = dot_nn(
            counts.astype(jnp.bfloat16), to_lane_low
        )
        out_ref[j * 4 * rows : (j + 1) * 4 * rows, :] = scratch[j].astype(jnp.bfloat16)


def dense_attention_kernel(
    in_ref, token_ref, out_ref, target_ref, stage, wide_ref, *, slots
):
    size = in_ref.shape[1]
    count = SOURCES * MESSAGE_ROWS
    wide = SOURCES * OWNED * WIDE
    sources = in_ref.shape[0] // (4 * MESSAGE_ROWS)
    steps = sources // SOURCES
    for s in range(sources):
        head_rows = in_ref[s * 4 * MESSAGE_ROWS : s * 4 * MESSAGE_ROWS + 16, :]
        stage[0, s : s + 1, :] = head_rows.astype(jnp.float32)[0:1]
    counts = stage[0, 0:sources, :]
    counts_low = counts.astype(jnp.bfloat16)
    most = jnp.max(jnp.sum(counts, axis=1, keepdims=True), axis=0, keepdims=True)
    overflow = jnp.broadcast_to(jnp.where(most > MESSAGE_ROWS - 1, 1.0, 0.0), (SOURCES, size))
    lane = lax.broadcasted_iota(jnp.int32, (size, wide), 1)
    lane_cluster = lane // WIDE % OWNED
    cluster = lax.broadcasted_iota(jnp.int32, (size, wide), 0)
    same = jnp.where(lane_cluster == cluster, 1.0, 0.0).astype(jnp.bfloat16)
    ahead = jnp.where(cluster < lane_cluster, 1.0, 0.0).astype(jnp.bfloat16)
    lane = lax.broadcasted_iota(jnp.int32, (sources, wide), 1)
    source = lax.broadcasted_iota(jnp.int32, (sources, wide), 0)
    slot = lane % WIDE
    spread = dot_nn(counts_low, same).astype(jnp.int32)
    target = dot_nn(counts_low, ahead).astype(jnp.int32) + slot + 1 + source % SOURCES * MESSAGE_ROWS
    live = jnp.logical_and(slot < spread, lane // (OWNED * WIDE) == source % SOURCES)
    steps_of = lax.broadcasted_iota(jnp.int32, (steps, sources), 1) // SOURCES == (
        lax.broadcasted_iota(jnp.int32, (steps, sources), 0)
    )
    target_ref[...] = dot_nn(
        jnp.where(steps_of, 1.0, 0.0).astype(jnp.bfloat16),
        jnp.where(live, target, 0).astype(jnp.float32).astype(jnp.bfloat16),
    ).astype(jnp.int32)
    slot_lane = lax.broadcasted_iota(jnp.int32, (sources, slots * sources), 1)
    repeat = lax.broadcasted_iota(jnp.int32, (sources, slots * sources), 0) == slot_lane % sources
    repeated = lax.dot_general(
        counts_low,
        jnp.where(repeat, 1.0, 0.0).astype(jnp.bfloat16),
        (((0,), (0,)), ((), ())),
        preferred_element_type=jnp.float32,
    )[:OWNED].astype(jnp.int32)
    keep = repeated > lax.broadcasted_iota(jnp.int32, (OWNED, slots * sources), 1) // sources
    row_ids = lax.broadcasted_iota(jnp.int32, (count, wide), 0)

    def selection(step):
        target = target_ref[pl.ds(step, 1), :]
        select = jnp.logical_and(row_ids == target, target > 0)
        return jnp.where(select, 1.0, 0.0).astype(jnp.bfloat16)

    def expand(pass_id, carry):
        for u in range(stage.shape[0]):
            step = pass_id * stage.shape[0] + u
            stage[u] = in_ref[pl.ds(step * 4 * count, 4 * count), :].astype(jnp.float32)
            parts = [stage[u, pl.ds(i, count, stride=4), :].astype(jnp.bfloat16) for i in range(4)]
            select = selection(step)
            into = pl.ds(step * wide, wide)
            query_key = dot_tn(select, jnp.concatenate(parts[:2], axis=1))
            value_grad = dot_tn(select, jnp.concatenate(parts[2:], axis=1))
            wide_ref[0, into, :] = query_key[:, :size]
            wide_ref[1, into, :] = query_key[:, size:]
            wide_ref[2, into, :] = value_grad[:, :size]
            wide_ref[3, into, :] = value_grad[:, size:]
        return carry

    def compact(pass_id, carry):
        for u in range(stage.shape[0]):
            step = pass_id * stage.shape[0] + u
            select = selection(step)
            parts = [
                wide_ref[i, pl.ds(step * wide, wide), :].astype(jnp.bfloat16) for i in range(4)
            ]
            first = dot_nn(select, jnp.concatenate(parts[:2], axis=1))
            second = dot_nn(select, jnp.concatenate(parts[2:], axis=1))
            stage[u, pl.ds(0, count, stride=4), :] = first[:, :size]
            stage[u, pl.ds(1, count, stride=4), :] = first[:, size:]
            stage[u, pl.ds(2, count, stride=4), :] = second[:, :size]
            stage[u, pl.ds(3, count, stride=4), :] = second[:, size:]
            stage[u, pl.ds(0, SOURCES, stride=4 * MESSAGE_ROWS), :] = overflow
            out_ref[pl.ds(step * 4 * count, 4 * count), :] = stage[u].astype(jnp.bfloat16)
        return carry

    lax.fori_loop(0, steps // stage.shape[0], expand, 0)
    for c in range(OWNED):
        spots = [pl.ds(c * WIDE + s, sources, stride=OWNED * WIDE) for s in range(slots)]
        tensors = [
            jnp.concatenate([wide_ref[i, spot, :] for spot in spots], axis=0).astype(jnp.bfloat16)
            for i in range(4)
        ]
        for i, result in enumerate(attend_cluster(*tensors, keep[c : c + 1])):
            for s, spot in enumerate(spots):
                wide_ref[i, spot, :] = result[s * sources : (s + 1) * sources]
    lax.fori_loop(0, steps // stage.shape[0], compact, 0)


def dense_unpack_kernel(place_ref, in_ref, o_ref, dq_ref, dk_ref, dv_ref, scratch):
    rows = scratch.shape[1] // 4
    group, _, tokens = place_ref.shape
    size = o_ref.shape[1] // group
    row_ids = lax.broadcasted_iota(jnp.int32, (rows, tokens), 0)
    for j in range(group):
        lanes = slice(j * size, (j + 1) * size)
        scratch[j] = in_ref[j * 4 * rows : (j + 1) * 4 * rows, :].astype(jnp.float32)
        select = jnp.where(row_ids == place_ref[j], 1.0, 0.0).astype(jnp.bfloat16)
        parts = [scratch[j, pl.ds(i, rows, stride=4), :].astype(jnp.bfloat16) for i in range(4)]
        first = dot_tn(select, jnp.concatenate(parts[:2], axis=1)).astype(jnp.bfloat16)
        second = dot_tn(select, jnp.concatenate(parts[2:], axis=1)).astype(jnp.bfloat16)
        o_ref[:, lanes] = first[:, :size]
        dq_ref[:, lanes] = first[:, size:]
        dk_ref[:, lanes] = second[:, :size]
        dv_ref[:, lanes] = second[:, size:]


def build(tokens, features, heads, owners):
    size = features // heads
    slots = 3 * tokens // (2 * owners)
    rows = owners * slots
    params = pltpu.CompilerParams(
        dimension_semantics=("arbitrary",), vmem_limit_bytes=40 * 1024 * 1024
    )
    packed_shape = jax.ShapeDtypeStruct((4 * rows, features), jnp.bfloat16)

    def head_rows(group):
        return pl.BlockSpec((tokens, group * size), lambda h: (0, h))

    def head_row(group):
        return pl.BlockSpec((group, 1, tokens), lambda h: (h, 0, 0))

    def packed_block(group):
        return pl.BlockSpec((4 * rows, group * size), lambda h: (0, h))

    def scratch(group):
        return pltpu.VMEM((group, 4 * rows, size), jnp.float32)

    pack = pl.pallas_call(
        lambda *refs: pack_kernel(*refs, owners=owners, slots=slots),
        grid=(heads // PACK_HEADS,),
        in_specs=[head_row(PACK_HEADS)] + [head_rows(PACK_HEADS)] * 4,
        out_specs=[packed_block(PACK_HEADS), head_row(PACK_HEADS)],
        out_shape=[packed_shape, jax.ShapeDtypeStruct((heads, 1, tokens), jnp.int32)],
        scratch_shapes=[scratch(PACK_HEADS)],
        compiler_params=params,
        name="pack_rows",
    )
    attend = pl.pallas_call(
        attention_kernel,
        grid=(heads // ATTEND_HEADS,),
        in_specs=[packed_block(ATTEND_HEADS)],
        out_specs=packed_block(ATTEND_HEADS),
        out_shape=packed_shape,
        scratch_shapes=[scratch(ATTEND_HEADS)] * 2,
        compiler_params=params,
        name="cluster_attention",
    )
    unpack = pl.pallas_call(
        unpack_kernel,
        grid=(heads // UNPACK_HEADS,),
        in_specs=[head_row(UNPACK_HEADS), packed_block(UNPACK_HEADS)],
        out_specs=[head_rows(UNPACK_HEADS)] * 4,
        out_shape=[jax.ShapeDtypeStruct((tokens, features), jnp.bfloat16)] * 4,
        scratch_shapes=[scratch(UNPACK_HEADS)],
        compiler_params=params,
        name="unpack_rows",
    )
    return pack, attend, unpack


def build_dense(tokens, features, heads, owners):
    size = features // heads
    clusters = heads * OWNED
    rows = OWNED * MESSAGE_ROWS
    slots = 3 * tokens // (2 * owners)
    params = pltpu.CompilerParams(
        dimension_semantics=("arbitrary",), vmem_limit_bytes=60 * 1024 * 1024
    )
    packed_shape = jax.ShapeDtypeStruct((heads * 4 * rows, size), jnp.bfloat16)

    def head_rows(group):
        return pl.BlockSpec((tokens, group * size), lambda h: (0, h))

    def head_row(group, length):
        return pl.BlockSpec((group, 1, length), lambda h: (h, 0, 0))

    def packed_block(group):
        return pl.BlockSpec((group * 4 * rows, size), lambda h: (h, 0))

    def scratch(group):
        return pltpu.VMEM((group, 4 * rows, size), jnp.float32)

    pack = pl.pallas_call(
        lambda *refs: dense_pack_kernel(*refs, clusters=clusters),
        grid=(heads // PACK_HEADS,),
        in_specs=[head_row(PACK_HEADS, tokens)] + [head_rows(PACK_HEADS)] * 4,
        out_specs=[
            packed_block(PACK_HEADS),
            head_row(PACK_HEADS, tokens),
        ],
        out_shape=[
            packed_shape,
            jax.ShapeDtypeStruct((heads, 1, tokens), jnp.int32),
        ],
        scratch_shapes=[scratch(PACK_HEADS)],
        compiler_params=params,
        name="dense_pack_rows",
    )
    attend = pl.pallas_call(
        lambda *refs: dense_attention_kernel(*refs, slots=slots),
        in_specs=[pl.BlockSpec(memory_space=pltpu.VMEM), pl.BlockSpec(memory_space=pl.ANY)],
        out_shape=packed_shape,
        scratch_shapes=[
            pltpu.VMEM((owners // SOURCES, SOURCES * OWNED * WIDE), jnp.int32),
            pltpu.VMEM((2, 4 * SOURCES * MESSAGE_ROWS, size), jnp.float32),
            pltpu.VMEM((4, owners * OWNED * WIDE, size), jnp.float32),
        ],
        compiler_params=pltpu.CompilerParams(vmem_limit_bytes=40 * 1024 * 1024),
        name="dense_cluster_attention",
    )
    unpack = pl.pallas_call(
        dense_unpack_kernel,
        grid=(heads // UNPACK_HEADS,),
        in_specs=[head_row(UNPACK_HEADS, tokens), packed_block(UNPACK_HEADS)],
        out_specs=[head_rows(UNPACK_HEADS)] * 4,
        out_shape=[jax.ShapeDtypeStruct((tokens, features), jnp.bfloat16)] * 4,
        scratch_shapes=[scratch(UNPACK_HEADS)],
        compiler_params=params,
        name="dense_unpack_rows",
    )
    return pack, attend, unpack


def exchange(packed, owners):
    moved = lax.all_to_all(
        packed.reshape(owners, -1, packed.shape[1]), "seq", split_axis=0, concat_axis=0, tiled=True
    )
    return moved.reshape(packed.shape)


def body(queries, key_rows, values, grad_out, routes):
    tokens, features = queries.shape
    heads = routes.shape[0]
    owners = lax.axis_size("seq")
    tensors = [
        pltpu.with_memory_space_constraint(array, pltpu.HBM)
        for array in (queries, key_rows, values, grad_out)
    ]
    routes = routes.reshape(heads, 1, tokens)
    pack, attend, unpack = build_dense(tokens, features, heads, owners)
    packed, place = pack(routes, *tensors)
    token = place[:, 0, :128]
    groups = lax.axis_size("head")
    turns = [
        (s * groups + h, (s + owners // 2 + 8) % owners * groups + h)
        for s in range(owners)
        for h in range(1, groups, 2)
    ]
    for _ in range(TOKEN_HOPS):
        token = jnp.maximum(token, lax.ppermute(token, ("seq", "head"), turns))
    packed, token = lax.optimization_barrier((packed, token))
    returned = exchange(attend(exchange(packed, owners), token), owners)
    overflow = jnp.max(returned.reshape(owners, -1, returned.shape[1])[:, 0, 0]) > 0.5

    def padded(place, returned, routes, *tensors):
        pack, attend, unpack = build(tokens, features, heads, owners)
        packed, place = pack(routes, *tensors)
        return tuple(unpack(place, exchange(attend(exchange(packed, owners)), owners)))

    def dense(place, returned, routes, *tensors):
        return tuple(unpack(place, returned))

    return lax.cond(overflow, padded, dense, place, returned, routes, *tensors)


def solution(mesh):
    in_specs = (
        P("seq", "head"),
        P("seq", "head"),
        P("seq", "head"),
        P("seq", "head"),
        P("head", "seq", None),
    )
    out_specs = (P("seq", "head"), P("seq", "head"), P("seq", "head"), P("seq", "head"))
    return jax.shard_map(body, mesh=mesh, in_specs=in_specs, out_specs=out_specs, check_vma=False)
```

```python
import math

import jax
import jax.numpy as jnp
from jax import lax
from jax.experimental import pallas as pl
from jax.experimental.pallas import tpu as pltpu
from jax.sharding import PartitionSpec as P

DEAD_KEY = 256.0
DEAD_TEST = 100.0
MESSAGE_ROWS = 44
OWNED = 8
WIDE = 8
SOURCES = 4
PACK_HEADS = 4
ATTEND_HEADS = 2
UNPACK_HEADS = 4
TOKEN_HOPS = 4


def dot_nn(left, right):
    return jnp.dot(left, right, preferred_element_type=jnp.float32)


def dot_nt(left, right):
    return lax.dot_general(left, right, (((1,), (1,)), ((), ())), preferred_element_type=jnp.float32)


def dot_tn(left, right):
    return lax.dot_general(left, right, (((0,), (0,)), ((), ())), preferred_element_type=jnp.float32)


def pack_kernel(routes_ref, q_ref, k_ref, v_ref, g_ref, out_ref, place_ref, scratch, *, owners, slots):
    group, _, tokens = routes_ref.shape
    rows = owners * slots
    size = q_ref.shape[1] // group
    earlier = lax.broadcasted_iota(jnp.int32, (tokens, tokens), 0) < lax.broadcasted_iota(
        jnp.int32, (tokens, tokens), 1
    )
    earlier_low = jnp.where(earlier, 1.0, 0.0).astype(jnp.bfloat16)
    owner_ids = lax.broadcasted_iota(jnp.int32, (owners, tokens), 0)
    row_ids = lax.broadcasted_iota(jnp.int32, (rows, tokens), 0)
    for j in range(group):
        lanes = slice(j * size, (j + 1) * size)
        clusters = routes_ref[j]
        onehot = owner_ids == clusters
        before = dot_nn(jnp.where(onehot, 1.0, 0.0).astype(jnp.bfloat16), earlier_low)
        ranking = jnp.sum(jnp.where(onehot, before, 0.0), axis=0, keepdims=True)
        place = clusters * slots + ranking.astype(jnp.int32)
        place_ref[j] = place
        select = jnp.where(row_ids == place, 1.0, 0.0).astype(jnp.bfloat16)
        query_key = dot_nn(select, jnp.concatenate([q_ref[:, lanes], k_ref[:, lanes]], axis=1))
        value_grad = dot_nn(select, jnp.concatenate([v_ref[:, lanes], g_ref[:, lanes]], axis=1))
        live = dot_nn(select, jnp.ones((tokens, size), jnp.bfloat16))
        scratch[j, pl.ds(0, rows, stride=4), :] = query_key[:, :size]
        scratch[j, pl.ds(1, rows, stride=4), :] = query_key[:, size:] + (1.0 - live) * DEAD_KEY
        scratch[j, pl.ds(2, rows, stride=4), :] = value_grad[:, :size]
        scratch[j, pl.ds(3, rows, stride=4), :] = value_grad[:, size:]
        out_ref[:, lanes] = scratch[j].astype(jnp.bfloat16)


def attend_cluster(query, key, value, grad, keep):
    size = query.shape[1]
    scaling = 1.0 / math.sqrt(size)
    scores = dot_nt(query, key) * scaling
    masked = jnp.where(keep, scores, -1e30)
    weights = jnp.exp(masked - jnp.max(masked, axis=1, keepdims=True))
    probability = weights * (1.0 / jnp.sum(weights, axis=1, keepdims=True))
    probability_low = probability.astype(jnp.bfloat16)
    output = dot_nn(probability_low, value).astype(jnp.bfloat16).astype(jnp.float32)
    grad_probability = dot_nt(grad, value)
    delta = jnp.sum(grad.astype(jnp.float32) * output, axis=1, keepdims=True)
    grad_scores = (probability * (grad_probability - delta)).astype(jnp.bfloat16)
    return (
        output,
        dot_nn(grad_scores, key) * scaling,
        dot_tn(grad_scores, query) * scaling,
        dot_tn(probability_low, grad),
    )


def attention_kernel(in_ref, out_ref, scratch, scratch_out):
    rows = in_ref.shape[0] // 4
    group = scratch.shape[0]
    size = in_ref.shape[1] // group
    for j in range(group):
        lanes = slice(j * size, (j + 1) * size)
        scratch[j] = in_ref[:, lanes].astype(jnp.float32)
        tensors = [scratch[j, pl.ds(i, rows, stride=4), :].astype(jnp.bfloat16) for i in range(4)]
        first_lane = jnp.where(lax.broadcasted_iota(jnp.int32, (8, size), 1) == 0, 1.0, 0.0)
        keep = dot_nt(first_lane.astype(jnp.bfloat16), tensors[1])[0:1] < DEAD_TEST
        for i, result in enumerate(attend_cluster(*tensors, keep)):
            scratch_out[j, pl.ds(i, rows, stride=4), :] = result
        out_ref[:, lanes] = scratch_out[j].astype(jnp.bfloat16)


def unpack_kernel(place_ref, in_ref, o_ref, dq_ref, dk_ref, dv_ref, scratch):
    rows = in_ref.shape[0] // 4
    group, _, tokens = place_ref.shape
    size = o_ref.shape[1] // group
    row_ids = lax.broadcasted_iota(jnp.int32, (rows, tokens), 0)
    for j in range(group):
        lanes = slice(j * size, (j + 1) * size)
        scratch[j] = in_ref[:, lanes].astype(jnp.float32)
        select = jnp.where(row_ids == place_ref[j], 1.0, 0.0).astype(jnp.bfloat16)
        parts = [scratch[j, pl.ds(i, rows, stride=4), :].astype(jnp.bfloat16) for i in range(4)]
        first = dot_tn(select, jnp.concatenate(parts[:2], axis=1)).astype(jnp.bfloat16)
        second = dot_tn(select, jnp.concatenate(parts[2:], axis=1)).astype(jnp.bfloat16)
        o_ref[:, lanes] = first[:, :size]
        dq_ref[:, lanes] = first[:, size:]
        dk_ref[:, lanes] = second[:, :size]
        dv_ref[:, lanes] = second[:, size:]


def dense_pack_kernel(
    routes_ref, q_ref, k_ref, v_ref, g_ref, out_ref, place_ref, scratch, *, clusters
):
    group, _, tokens = routes_ref.shape
    rows = scratch.shape[1] // 4
    size = q_ref.shape[1] // group
    octets = clusters // OWNED
    earlier = lax.broadcasted_iota(jnp.int32, (tokens, tokens), 0) < lax.broadcasted_iota(
        jnp.int32, (tokens, tokens), 1
    )
    earlier_low = jnp.where(earlier, 1.0, 0.0).astype(jnp.bfloat16)
    this = lax.broadcasted_iota(jnp.int32, (clusters, clusters), 0)
    other = lax.broadcasted_iota(jnp.int32, (clusters, clusters), 1)
    lower = jnp.logical_and(other < this, other // OWNED == this // OWNED)
    lower_low = jnp.where(lower, 1.0, 0.0).astype(jnp.bfloat16)
    all_tokens = jnp.ones((tokens, tokens), jnp.bfloat16)
    cluster_ids = lax.broadcasted_iota(jnp.int32, (clusters, tokens), 0)
    row_ids = lax.broadcasted_iota(jnp.int32, (rows, tokens), 0)
    in_octet = lax.broadcasted_iota(jnp.int32, (octets, clusters), 1) // OWNED == (
        lax.broadcasted_iota(jnp.int32, (octets, clusters), 0)
    )
    to_lane = lax.broadcasted_iota(jnp.int32, (clusters, size), 0) % OWNED == (
        lax.broadcasted_iota(jnp.int32, (clusters, size), 1)
    )
    to_lane_low = jnp.where(to_lane, 1.0, 0.0).astype(jnp.bfloat16)
    for j in range(group):
        lanes = slice(j * size, (j + 1) * size)
        route = routes_ref[j]
        onehot = cluster_ids == route
        onehot_low = jnp.where(onehot, 1.0, 0.0).astype(jnp.bfloat16)
        counts = dot_nt(all_tokens[:octets], onehot_low)
        counts = jnp.where(in_octet, counts, 0.0)
        in_lower = dot_nn(lower_low, onehot_low).astype(jnp.bfloat16)
        before = dot_nn(onehot_low, earlier_low) + dot_nn(in_lower, all_tokens)
        ranking = jnp.sum(jnp.where(onehot, before, 0.0), axis=0, keepdims=True)
        place = route // OWNED * MESSAGE_ROWS + 1 + ranking.astype(jnp.int32)
        place_ref[j] = place
        select = jnp.where(row_ids == place, 1.0, 0.0).astype(jnp.bfloat16)
        query_key = dot_nn(select, jnp.concatenate([q_ref[:, lanes], k_ref[:, lanes]], axis=1))
        value_grad = dot_nn(select, jnp.concatenate([v_ref[:, lanes], g_ref[:, lanes]], axis=1))
        scratch[j, pl.ds(0, rows, stride=4), :] = query_key[:, :size]
        scratch[j, pl.ds(1, rows, stride=4), :] = query_key[:, size:]
        scratch[j, pl.ds(2, rows, stride=4), :] = value_grad[:, :size]
        scratch[j, pl.ds(3, rows, stride=4), :] = value_grad[:, size:]
        scratch[j, pl.ds(0, octets, stride=4 * MESSAGE_ROWS), :] = dot_nn(
            counts.astype(jnp.bfloat16), to_lane_low
        )
        out_ref[j * 4 * rows : (j + 1) * 4 * rows, :] = scratch[j].astype(jnp.bfloat16)


def dense_attention_kernel(
    in_ref, token_ref, out_ref, target_ref, stage, wide_ref, *, slots
):
    size = in_ref.shape[1]
    count = SOURCES * MESSAGE_ROWS
    wide = SOURCES * OWNED * WIDE
    sources = in_ref.shape[0] // (4 * MESSAGE_ROWS)
    steps = sources // SOURCES
    for s in range(sources):
        head_rows = in_ref[s * 4 * MESSAGE_ROWS : s * 4 * MESSAGE_ROWS + 16, :]
        stage[0, s : s + 1, :] = head_rows.astype(jnp.float32)[0:1]
    counts = stage[0, 0:sources, :]
    counts_low = counts.astype(jnp.bfloat16)
    most = jnp.max(jnp.sum(counts, axis=1, keepdims=True), axis=0, keepdims=True)
    overflow = jnp.broadcast_to(jnp.where(most > MESSAGE_ROWS - 1, 1.0, 0.0), (SOURCES, size))
    lane = lax.broadcasted_iota(jnp.int32, (size, wide), 1)
    lane_cluster = lane // WIDE % OWNED
    cluster = lax.broadcasted_iota(jnp.int32, (size, wide), 0)
    same = jnp.where(lane_cluster == cluster, 1.0, 0.0).astype(jnp.bfloat16)
    ahead = jnp.where(cluster < lane_cluster, 1.0, 0.0).astype(jnp.bfloat16)
    lane = lax.broadcasted_iota(jnp.int32, (sources, wide), 1)
    source = lax.broadcasted_iota(jnp.int32, (sources, wide), 0)
    slot = lane % WIDE
    spread = dot_nn(counts_low, same).astype(jnp.int32)
    target = dot_nn(counts_low, ahead).astype(jnp.int32) + slot + 1 + source % SOURCES * MESSAGE_ROWS
    live = jnp.logical_and(slot < spread, lane // (OWNED * WIDE) == source % SOURCES)
    steps_of = lax.broadcasted_iota(jnp.int32, (steps, sources), 1) // SOURCES == (
        lax.broadcasted_iota(jnp.int32, (steps, sources), 0)
    )
    target_ref[...] = dot_nn(
        jnp.where(steps_of, 1.0, 0.0).astype(jnp.bfloat16),
        jnp.where(live, target, 0).astype(jnp.float32).astype(jnp.bfloat16),
    ).astype(jnp.int32)
    slot_lane = lax.broadcasted_iota(jnp.int32, (sources, slots * sources), 1)
    repeat = lax.broadcasted_iota(jnp.int32, (sources, slots * sources), 0) == slot_lane % sources
    repeated = lax.dot_general(
        counts_low,
        jnp.where(repeat, 1.0, 0.0).astype(jnp.bfloat16),
        (((0,), (0,)), ((), ())),
        preferred_element_type=jnp.float32,
    )[:OWNED].astype(jnp.int32)
    keep = repeated > lax.broadcasted_iota(jnp.int32, (OWNED, slots * sources), 1) // sources
    row_ids = lax.broadcasted_iota(jnp.int32, (count, wide), 0)

    def selection(step):
        target = target_ref[pl.ds(step, 1), :]
        select = jnp.logical_and(row_ids == target, target > 0)
        return jnp.where(select, 1.0, 0.0).astype(jnp.bfloat16)

    def expand(pass_id, carry):
        for u in range(stage.shape[0]):
            step = pass_id * stage.shape[0] + u
            stage[u] = in_ref[pl.ds(step * 4 * count, 4 * count), :].astype(jnp.float32)
            parts = [stage[u, pl.ds(i, count, stride=4), :].astype(jnp.bfloat16) for i in range(4)]
            select = selection(step)
            into = pl.ds(step * wide, wide)
            query_key = dot_tn(select, jnp.concatenate(parts[:2], axis=1))
            value_grad = dot_tn(select, jnp.concatenate(parts[2:], axis=1))
            wide_ref[0, into, :] = query_key[:, :size]
            wide_ref[1, into, :] = query_key[:, size:]
            wide_ref[2, into, :] = value_grad[:, :size]
            wide_ref[3, into, :] = value_grad[:, size:]
        return carry

    def compact(pass_id, carry):
        for u in range(stage.shape[0]):
            step = pass_id * stage.shape[0] + u
            select = selection(step)
            parts = [
                wide_ref[i, pl.ds(step * wide, wide), :].astype(jnp.bfloat16) for i in range(4)
            ]
            first = dot_nn(select, jnp.concatenate(parts[:2], axis=1))
            second = dot_nn(select, jnp.concatenate(parts[2:], axis=1))
            stage[u, pl.ds(0, count, stride=4), :] = first[:, :size]
            stage[u, pl.ds(1, count, stride=4), :] = first[:, size:]
            stage[u, pl.ds(2, count, stride=4), :] = second[:, :size]
            stage[u, pl.ds(3, count, stride=4), :] = second[:, size:]
            stage[u, pl.ds(0, SOURCES, stride=4 * MESSAGE_ROWS), :] = overflow
            out_ref[pl.ds(step * 4 * count, 4 * count), :] = stage[u].astype(jnp.bfloat16)
        return carry

    lax.fori_loop(0, steps // stage.shape[0], expand, 0)
    for c in range(OWNED):
        spots = [pl.ds(c * WIDE + s, sources, stride=OWNED * WIDE) for s in range(slots)]
        tensors = [
            jnp.concatenate([wide_ref[i, spot, :] for spot in spots], axis=0).astype(jnp.bfloat16)
            for i in range(4)
        ]
        for i, result in enumerate(attend_cluster(*tensors, keep[c : c + 1])):
            for s, spot in enumerate(spots):
                wide_ref[i, spot, :] = result[s * sources : (s + 1) * sources]
    lax.fori_loop(0, steps // stage.shape[0], compact, 0)


def dense_unpack_kernel(place_ref, in_ref, o_ref, dq_ref, dk_ref, dv_ref, scratch):
    rows = scratch.shape[1] // 4
    group, _, tokens = place_ref.shape
    size = o_ref.shape[1] // group
    row_ids = lax.broadcasted_iota(jnp.int32, (rows, tokens), 0)
    for j in range(group):
        lanes = slice(j * size, (j + 1) * size)
        scratch[j] = in_ref[j * 4 * rows : (j + 1) * 4 * rows, :].astype(jnp.float32)
        select = jnp.where(row_ids == place_ref[j], 1.0, 0.0).astype(jnp.bfloat16)
        parts = [scratch[j, pl.ds(i, rows, stride=4), :].astype(jnp.bfloat16) for i in range(4)]
        first = dot_tn(select, jnp.concatenate(parts[:2], axis=1)).astype(jnp.bfloat16)
        second = dot_tn(select, jnp.concatenate(parts[2:], axis=1)).astype(jnp.bfloat16)
        o_ref[:, lanes] = first[:, :size]
        dq_ref[:, lanes] = first[:, size:]
        dk_ref[:, lanes] = second[:, :size]
        dv_ref[:, lanes] = second[:, size:]


def build(tokens, features, heads, owners):
    size = features // heads
    slots = 3 * tokens // (2 * owners)
    rows = owners * slots
    params = pltpu.CompilerParams(
        dimension_semantics=("arbitrary",), vmem_limit_bytes=40 * 1024 * 1024
    )
    packed_shape = jax.ShapeDtypeStruct((4 * rows, features), jnp.bfloat16)

    def head_rows(group):
        return pl.BlockSpec((tokens, group * size), lambda h: (0, h))

    def head_row(group):
        return pl.BlockSpec((group, 1, tokens), lambda h: (h, 0, 0))

    def packed_block(group):
        return pl.BlockSpec((4 * rows, group * size), lambda h: (0, h))

    def scratch(group):
        return pltpu.VMEM((group, 4 * rows, size), jnp.float32)

    pack = pl.pallas_call(
        lambda *refs: pack_kernel(*refs, owners=owners, slots=slots),
        grid=(heads // PACK_HEADS,),
        in_specs=[head_row(PACK_HEADS)] + [head_rows(PACK_HEADS)] * 4,
        out_specs=[packed_block(PACK_HEADS), head_row(PACK_HEADS)],
        out_shape=[packed_shape, jax.ShapeDtypeStruct((heads, 1, tokens), jnp.int32)],
        scratch_shapes=[scratch(PACK_HEADS)],
        compiler_params=params,
        name="pack_rows",
    )
    attend = pl.pallas_call(
        attention_kernel,
        grid=(heads // ATTEND_HEADS,),
        in_specs=[packed_block(ATTEND_HEADS)],
        out_specs=packed_block(ATTEND_HEADS),
        out_shape=packed_shape,
        scratch_shapes=[scratch(ATTEND_HEADS)] * 2,
        compiler_params=params,
        name="cluster_attention",
    )
    unpack = pl.pallas_call(
        unpack_kernel,
        grid=(heads // UNPACK_HEADS,),
        in_specs=[head_row(UNPACK_HEADS), packed_block(UNPACK_HEADS)],
        out_specs=[head_rows(UNPACK_HEADS)] * 4,
        out_shape=[jax.ShapeDtypeStruct((tokens, features), jnp.bfloat16)] * 4,
        scratch_shapes=[scratch(UNPACK_HEADS)],
        compiler_params=params,
        name="unpack_rows",
    )
    return pack, attend, unpack


def build_dense(tokens, features, heads, owners):
    size = features // heads
    clusters = heads * OWNED
    rows = OWNED * MESSAGE_ROWS
    slots = 3 * tokens // (2 * owners)
    params = pltpu.CompilerParams(
        dimension_semantics=("arbitrary",), vmem_limit_bytes=60 * 1024 * 1024
    )
    packed_shape = jax.ShapeDtypeStruct((heads * 4 * rows, size), jnp.bfloat16)

    def head_rows(group):
        return pl.BlockSpec((tokens, group * size), lambda h: (0, h))

    def head_row(group, length):
        return pl.BlockSpec((group, 1, length), lambda h: (h, 0, 0))

    def packed_block(group):
        return pl.BlockSpec((group * 4 * rows, size), lambda h: (h, 0))

    def scratch(group):
        return pltpu.VMEM((group, 4 * rows, size), jnp.float32)

    pack = pl.pallas_call(
        lambda *refs: dense_pack_kernel(*refs, clusters=clusters),
        grid=(heads // PACK_HEADS,),
        in_specs=[head_row(PACK_HEADS, tokens)] + [head_rows(PACK_HEADS)] * 4,
        out_specs=[
            packed_block(PACK_HEADS),
            head_row(PACK_HEADS, tokens),
        ],
        out_shape=[
            packed_shape,
            jax.ShapeDtypeStruct((heads, 1, tokens), jnp.int32),
        ],
        scratch_shapes=[scratch(PACK_HEADS)],
        compiler_params=params,
        name="dense_pack_rows",
    )
    attend = pl.pallas_call(
        lambda *refs: dense_attention_kernel(*refs, slots=slots),
        in_specs=[pl.BlockSpec(memory_space=pltpu.VMEM), pl.BlockSpec(memory_space=pl.ANY)],
        out_shape=packed_shape,
        scratch_shapes=[
            pltpu.VMEM((owners // SOURCES, SOURCES * OWNED * WIDE), jnp.int32),
            pltpu.VMEM((2, 4 * SOURCES * MESSAGE_ROWS, size), jnp.float32),
            pltpu.VMEM((4, owners * OWNED * WIDE, size), jnp.float32),
        ],
        compiler_params=pltpu.CompilerParams(vmem_limit_bytes=40 * 1024 * 1024),
        name="dense_cluster_attention",
    )
    unpack = pl.pallas_call(
        dense_unpack_kernel,
        grid=(heads // UNPACK_HEADS,),
        in_specs=[head_row(UNPACK_HEADS, tokens), packed_block(UNPACK_HEADS)],
        out_specs=[head_rows(UNPACK_HEADS)] * 4,
        out_shape=[jax.ShapeDtypeStruct((tokens, features), jnp.bfloat16)] * 4,
        scratch_shapes=[scratch(UNPACK_HEADS)],
        compiler_params=params,
        name="dense_unpack_rows",
    )
    return pack, attend, unpack


def exchange(packed, owners):
    moved = lax.all_to_all(
        packed.reshape(owners, -1, packed.shape[1]), "seq", split_axis=0, concat_axis=0, tiled=True
    )
    return moved.reshape(packed.shape)


def body(queries, key_rows, values, grad_out, routes):
    tokens, features = queries.shape
    heads = routes.shape[0]
    owners = lax.axis_size("seq")
    tensors = [
        pltpu.with_memory_space_constraint(array, pltpu.HBM)
        for array in (queries, key_rows, values, grad_out)
    ]
    routes = routes.reshape(heads, 1, tokens)
    pack, attend, unpack = build_dense(tokens, features, heads, owners)
    packed, place = pack(routes, *tensors)
    token = place[:, 0, :128]
    groups = lax.axis_size("head")
    turns = [
        (s * groups + h, (s + owners // 2 + 8) % owners * groups + h)
        for s in range(owners)
        for h in range(1, groups, 2)
    ]
    for _ in range(TOKEN_HOPS):
        token = jnp.maximum(token, lax.ppermute(token, ("seq", "head"), turns))
    packed, token = lax.optimization_barrier((packed, token))
    returned = exchange(attend(exchange(packed, owners), token), owners)
    overflow = jnp.max(returned.reshape(owners, -1, returned.shape[1])[:, 0, 0]) > 0.5

    def padded(place, returned, routes, *tensors):
        pack, attend, unpack = build(tokens, features, heads, owners)
        packed, place = pack(routes, *tensors)
        return tuple(unpack(place, exchange(attend(exchange(packed, owners)), owners)))

    def dense(place, returned, routes, *tensors):
        return tuple(unpack(place, returned))

    return lax.cond(overflow, padded, dense, place, returned, routes, *tensors)


def solution(mesh):
    in_specs = (
        P("seq", "head"),
        P("seq", "head"),
        P("seq", "head"),
        P("seq", "head"),
        P("head", "seq", None),
    )
    out_specs = (P("seq", "head"), P("seq", "head"), P("seq", "head"), P("seq", "head"))
    return jax.shard_map(body, mesh=mesh, in_specs=in_specs, out_specs=out_specs, check_vma=False)
```
